512 devices in a mesh: seq: 32 (over x, y), head: 16 (over z, core).
Axes of the slice: x: 4, y: 8, z: 8, core: 2. Of those that a mesh axis runs over, the one named last changes fastest.
Arguments:
- queries: bfloat16 [65536, 2048], P(('seq', 'head')), may hold values from -6 to 6
- keys: bfloat16 [65536, 2048], P(('seq', 'head')), may hold values from -6 to 6
- values: bfloat16 [65536, 2048], P(('seq', 'head')), may hold values from -6 to 6
- log_decay: bfloat16 [65536, 16], P(('seq', 'head')), may hold values from -0.6 to 0, as said below
- out_weight: bfloat16 [2048, 2048], P(('seq', 'head')), may hold values from -0.125 to 0.125
Outputs:
- mixed_out: bfloat16 [65536, 2048], P(('seq', 'head'))
The draws below stay inside these ranges and needn't reach their ends.
Inputs may be any that keep to these rules, and one draw needn't show every extreme that they name: `log_decay`: every entry is at most zero.
All inputs are finite; a program needn't handle non-finite values.
Results may differ from the reference program's by a relative error of at most 0.0054.
Values may be sent and summed in bfloat16 or wider, within the bound.
No kernel may reach another device: no remote copies, remote signals or barrier semaphores. Data moves between devices by JAX's collectives and lax.ppermute only.
A program may use at most 64 MiB of HBM per device.

```python
import math
import jax
import jax.numpy as jnp
from jax import lax

H = 16
HD = 128
D = 2048
SPAN = 256
TOKENS = 65536


def draw_log_decay(key, part):
    key_heads, key_rates, key_noise, key_spots, key_depth = jax.random.split(jax.random.fold_in(key, 11), 5)
    order = jax.random.permutation(key_heads, H)
    fast_count = H // 2
    is_fast = order < fast_count
    spread = jax.random.uniform(key_rates, (H,), jnp.float32, 0.0, 1.0)
    fast_rate = jnp.exp(math.log(1.0 / 60.0) + spread * math.log(3.0))
    slow_rate = jnp.exp(math.log(0.2) + spread * math.log(3.0)) / TOKENS
    rate = jnp.where(is_fast, fast_rate, slow_rate)
    noise = jnp.exp(jax.random.uniform(key_noise, (TOKENS, H), jnp.float32, -math.log(2.0), math.log(2.0)))
    spots = jax.random.randint(key_spots, (3,), 0, TOKENS)
    positions = lax_iota(TOKENS)
    struck = jnp.any(positions[:, None] == spots[None, :], axis=1)
    depth = jax.random.uniform(key_depth, (TOKENS, 1), jnp.float32, 0.22, 0.5)
    result = -(rate[None, :] * noise) - jnp.where(struck[:, None], depth, 0.0)
    return result.astype(jnp.bfloat16)


def lax_iota(length):
    return jnp.arange(length, dtype=jnp.int32)


def shard_levels(key, shape, cuts, least, top_value):
    gain = 1.0
    for position, shards_of in cuts:
        heights = jax.random.uniform(jax.random.fold_in(jax.random.fold_in(key, 6), position), (shards_of,), jnp.float32, least / len(cuts), top_value / len(cuts))
        gain = gain * jnp.repeat(jnp.exp(heights), shape[position] // shards_of).reshape((-1,) + (1,) * (len(shape) - 1 - position))
    return gain


def bell_draw(stream_key, shape, width, bound, cuts=(), kind=jnp.bfloat16):
    entries = width * jax.random.normal(stream_key, shape, jnp.float32)
    if cuts:
        entries = entries * shard_levels(stream_key, shape, cuts, -0.22, 0.18)
    return jnp.clip(entries, -bound, bound).astype(kind)


def setup_inputs(seed: int = 0) -> dict:
    splits = jax.random.split(jax.random.key(seed), 6)
    queries = bell_draw(splits[0], (TOKENS, D), 1.0, 6.0, ((0, 512),))
    keys = bell_draw(splits[1], (TOKENS, D), 1.0, 6.0, ((0, 512),))
    values = bell_draw(splits[2], (TOKENS, D), 1.0, 6.0, ((0, 512),))
    log_decay = draw_log_decay(jax.random.fold_in(splits[5], 71), 0)
    out_weight = bell_draw(splits[4], (D, D), D ** -0.5, 0.125, ((0, 512),))
    return dict(queries=queries, keys=keys, values=values, log_decay=log_decay, out_weight=out_weight)


def reference(queries, keys, values, log_decay, out_weight):
    block_count = TOKENS // SPAN
    queries_blk = queries.reshape(block_count, SPAN, H, HD)
    keys_blk = keys.reshape(block_count, SPAN, H, HD)
    values_blk = values.reshape(block_count, SPAN, H, HD)
    decay_blk = log_decay.reshape(block_count, SPAN, H)
    causal = lax.broadcasted_iota(jnp.int32, (SPAN, SPAN), 0) >= lax.broadcasted_iota(jnp.int32, (SPAN, SPAN), 1)

    def advance(state_now, inputs):
        query_part, key_part, value_part, decay_part = inputs
        within = jnp.cumsum(decay_part.astype(jnp.float32), axis=0)
        block_decay = within[-1]
        within_t = within.T
        differences = within_t[:, :, None] - within_t[:, None, :]
        decay_mask = jnp.exp(jnp.where(causal[None], differences, -jnp.inf))
        query_f = query_part.astype(jnp.float32)
        key_f = key_part.astype(jnp.float32)
        value_f = value_part.astype(jnp.float32)
        scores = jnp.einsum('thd,shd->hts', query_f, key_f)
        weights = (scores * decay_mask).astype(jnp.bfloat16)
        local_part = jnp.einsum('hts,shd->thd', weights.astype(jnp.float32), value_f)
        scaled_keys = (jnp.exp(block_decay[None, :] - within)[:, :, None] * key_f).astype(jnp.bfloat16)
        block_state = jnp.einsum('shd,she->hde', scaled_keys.astype(jnp.float32), value_f)
        scaled_queries = query_f * jnp.exp(within)[:, :, None]
        carried_part = jnp.einsum('thd,hde->the', scaled_queries, state_now, precision=lax.Precision.HIGHEST)
        combined = local_part + carried_part
        normed = combined * lax.rsqrt(lax.optimization_barrier(jnp.mean(combined * combined, axis=-1, keepdims=True)) + 1e-05)
        state_next = jnp.exp(block_decay)[:, None, None] * state_now + block_state
        return (state_next, normed.astype(jnp.bfloat16))
    initial = jnp.zeros((H, HD, HD), jnp.float32)
    _, normed_all = lax.scan(advance, initial, (queries_blk, keys_blk, values_blk, decay_blk))
    normed_all = normed_all.reshape(TOKENS, D)
    return jnp.dot(normed_all, out_weight, preferred_element_type=jnp.float32).astype(jnp.bfloat16)
```

```python
import jax
import jax.numpy as jnp
from jax import lax
from jax.experimental import pallas as pl
from jax.experimental.pallas import tpu as pltpu
from jax.sharding import PartitionSpec as P

HD = 128
PAD = 8
BF16 = jnp.bfloat16
F32 = jnp.float32
VMEM = pltpu.CompilerParams(vmem_limit_bytes=40 * 1024 * 1024)


def ones_below(rows):
    return (
        lax.broadcasted_iota(jnp.int32, (rows, rows), 0)
        >= lax.broadcasted_iota(jnp.int32, (rows, rows), 1)
    ).astype(BF16)


def dot(a, b, ca, cb):
    return lax.dot_general(a, b, (((ca,), (cb,)), ((), ())), preferred_element_type=F32)


def within_rows(decay_t):
    return dot(decay_t, ones_below(decay_t.shape[1]), 1, 1)


def within_cols(decay_t):
    return dot(ones_below(decay_t.shape[1]), decay_t, 1, 1)


def states_kernel(decay_ref, keys_ref, values_ref, out_ref):
    heads, count = decay_ref.shape
    within = within_rows(decay_ref[...])
    total = within[:, count - 1 : count]
    coef = jnp.exp(total - within)
    row = lax.broadcasted_iota(jnp.int32, (PAD, HD), 0)
    for h in range(heads):
        cols = slice(h * HD, (h + 1) * HD)
        keys_t = keys_ref[:, cols].astype(F32).T * coef[h : h + 1, :]
        state = dot(keys_t.astype(BF16), values_ref[:, cols], 1, 0)
        out_ref[h, :HD, :] = state.astype(BF16)
        whole = jnp.broadcast_to(total[h : h + 1, :], (PAD, HD))
        high = whole.astype(BF16).astype(F32)
        middle = (whole - high).astype(BF16).astype(F32)
        low = whole - high - middle
        parts = jnp.where(row == 0, high, jnp.where(row == 1, middle, jnp.where(row == 2, low, 0.0)))
        out_ref[h, HD:, :] = parts.astype(BF16)


def total_of(ref, i):
    parts = ref[i, HD:, :].astype(F32)
    return parts[0:1, :] + parts[1:2, :] + parts[2:3, :]


def group_kernel(group_ref, out_ref, work_ref):
    chunks = out_ref.shape[0]
    rows = HD // chunks
    state = jnp.zeros((HD, HD), F32)
    total = jnp.zeros((1, HD), F32)
    for i in range(group_ref.shape[0]):
        step = total_of(group_ref, i)
        state = jnp.exp(step) * state + group_ref[i, :HD, :].astype(F32)
        total = total + step
    work_ref[...] = state
    for j in range(chunks):
        out_ref[j, :rows, :] = work_ref[rows * j : rows * (j + 1), :]
        out_ref[j, rows:, :] = jnp.broadcast_to(total, (PAD - rows, HD))


def scan_kernel(in_ref, out_ref):
    rows = out_ref.shape[1]
    state = jnp.zeros((rows, HD), F32)
    for i in range(in_ref.shape[0]):
        out_ref[i] = state
        state = jnp.exp(in_ref[i, rows : rows + 1, :]) * state + in_ref[i, :rows, :]


def prior_kernel(chunks_ref, group_ref, out_ref, work_ref):
    chunks, rows, _ = chunks_ref.shape
    for j in range(chunks):
        work_ref[rows * j : rows * (j + 1), :] = chunks_ref[j]
    state = work_ref[...]
    for i in range(group_ref.shape[0]):
        out_ref[i] = state.astype(BF16)
        state = jnp.exp(total_of(group_ref, i)) * state + group_ref[i, :HD, :].astype(F32)


def local_kernel(decay_ref, queries_ref, keys_ref, values_ref, out_ref):
    heads, count = decay_ref.shape
    rows = within_rows(decay_ref[...])
    cols = within_cols(decay_ref[...])
    causal = lax.broadcasted_iota(jnp.int32, (count, count), 0) >= lax.broadcasted_iota(
        jnp.int32, (count, count), 1
    )
    for h in range(heads):
        part = slice(h * HD, (h + 1) * HD)
        scores = dot(queries_ref[:, part], keys_ref[:, part], 1, 1)
        gaps = cols[:, h : h + 1] - rows[h : h + 1, :]
        decay = jnp.exp(jnp.where(causal, gaps, -jnp.inf))
        weights = (scores * decay).astype(BF16)
        out_ref[:, part] = dot(weights, values_ref[:, part], 1, 0)


def norm_kernel(decay_ref, queries_ref, local_ref, prior_ref, out_ref):
    heads = decay_ref.shape[0]
    scale = jnp.exp(within_cols(decay_ref[...]))
    place = lax.broadcasted_iota(jnp.int32, (HD, HD), 1)
    source = lax.broadcasted_iota(jnp.int32, (HD, HD), 0)
    quarter = HD // 8
    wanted = (place // 4 % 2) * (4 * quarter) + (place // 8) * 4 + place % 4
    reorder = (source == wanted).astype(BF16)
    for h in range(heads):
        part = slice(h * HD, (h + 1) * HD)
        carried = dot(queries_ref[:, part], prior_ref[h], 1, 0) * scale[:, h : h + 1]
        combined = local_ref[:, part] + carried
        square = jnp.mean(combined * combined, axis=-1, keepdims=True)
        normed = (combined * lax.rsqrt(square + 1e-05)).astype(BF16)
        out_ref[:, part] = dot(normed, reorder, 1, 0).astype(BF16)


def project_kernel(normed_ref, weight_ref, out_ref, rows_ref, sems):
    heads = weight_ref.shape[1]

    def copy(h):
        return pltpu.make_async_copy(weight_ref.at[:, h], rows_ref.at[h], sems.at[h])

    for h in range(heads):
        copy(h).start()
    acc = jnp.zeros(out_ref.shape, F32)
    for h in range(0, heads, 2):
        copy(h).wait()
        copy(h + 1).wait()
        rows = rows_ref[h : h + 2].reshape(2 * HD, out_ref.shape[1])
        acc = acc + dot(normed_ref[:, h * HD : (h + 2) * HD], rows, 1, 0)
    out_ref[...] = acc.astype(BF16)


def shape(*dims, kind=F32):
    return jax.ShapeDtypeStruct(dims, kind)


def mix(queries, keys, values, log_decay, out_weight):
    count, width = queries.shape
    heads = log_decay.shape[1]
    groups = lax.axis_size("seq")
    members = lax.axis_size("head")
    decay_t = log_decay.T

    weight_rows = out_weight.shape[0]
    spread = jnp.broadcast_to(out_weight[None], (groups, weight_rows, width))
    spread = lax.all_to_all(spread, "seq", split_axis=0, concat_axis=0, tiled=True)
    spread = spread.reshape(groups * weight_rows, width)
    weight = lax.all_gather(spread, "head", axis=0, tiled=True)

    own = pl.pallas_call(
        states_kernel, out_shape=shape(heads, HD + PAD, HD, kind=BF16), compiler_params=VMEM
    )(decay_t, keys, values)
    group = lax.all_to_all(own, "head", split_axis=0, concat_axis=0, tiled=True)
    local_part = pl.pallas_call(
        local_kernel, out_shape=shape(count, width), compiler_params=VMEM
    )(decay_t, queries, keys, values)
    chunks = pl.pallas_call(
        group_kernel,
        out_shape=shape(groups, PAD, HD),
        scratch_shapes=[pltpu.VMEM((HD, HD), F32)],
        compiler_params=VMEM,
    )(group)
    chunks = lax.all_to_all(chunks, "seq", split_axis=0, concat_axis=0, tiled=True)
    chunks = pl.pallas_call(
        scan_kernel, out_shape=shape(groups, HD // groups, HD), compiler_params=VMEM
    )(chunks)
    chunks = lax.all_to_all(chunks, "seq", split_axis=0, concat_axis=0, tiled=True)
    prior = pl.pallas_call(
        prior_kernel,
        out_shape=shape(members, HD, HD, kind=BF16),
        scratch_shapes=[pltpu.VMEM((HD, HD), F32)],
        compiler_params=VMEM,
    )(chunks, group)
    prior = lax.all_to_all(prior, "head", split_axis=0, concat_axis=0, tiled=True)
    normed = pl.pallas_call(
        norm_kernel, out_shape=shape(count, width, kind=BF16), compiler_params=VMEM
    )(decay_t, queries, local_part, prior)
    runs = 2 * weight_rows
    weight = weight.reshape(members, groups // 2, runs, width)
    weight = pltpu.with_memory_space_constraint(weight, pltpu.HBM)
    vmem = pl.BlockSpec(memory_space=pltpu.VMEM)
    return pl.pallas_call(
        project_kernel,
        out_shape=shape(count, width, kind=BF16),
        in_specs=[vmem, pl.BlockSpec(memory_space=pltpu.HBM)],
        out_specs=vmem,
        scratch_shapes=[
            pltpu.VMEM((heads, members, runs, width), BF16),
            pltpu.SemaphoreType.DMA((heads,)),
        ],
        compiler_params=VMEM,
    )(normed, weight)


def solution(mesh):
    placed = P(("seq", "head"), None)
    return jax.shard_map(mix, mesh=mesh, in_specs=(placed,) * 5, out_specs=placed, check_vma=False)
```

```python
import jax
import jax.numpy as jnp
from jax import lax
from jax.experimental import pallas as pl
from jax.experimental.pallas import tpu as pltpu
from jax.sharding import PartitionSpec as P

HD = 128
PAD = 8
NEAR = 32
BF16 = jnp.bfloat16
F32 = jnp.float32
VMEM = pltpu.CompilerParams(vmem_limit_bytes=40 * 1024 * 1024)


def ones_below(rows):
    return (
        lax.broadcasted_iota(jnp.int32, (rows, rows), 0)
        >= lax.broadcasted_iota(jnp.int32, (rows, rows), 1)
    ).astype(BF16)


def dot(a, b, ca, cb):
    return lax.dot_general(a, b, (((ca,), (cb,)), ((), ())), preferred_element_type=F32)


def within_rows(decay_t):
    return dot(decay_t, ones_below(decay_t.shape[1]), 1, 1)


def within_cols(decay_t):
    return dot(ones_below(decay_t.shape[1]), decay_t, 1, 1)


def parts_of(total):
    row = lax.broadcasted_iota(jnp.int32, (PAD, HD), 0)
    whole = jnp.broadcast_to(total, (PAD, HD))
    high = whole.astype(BF16).astype(F32)
    middle = (whole - high).astype(BF16).astype(F32)
    low = whole - high - middle
    parts = jnp.where(row == 0, high, jnp.where(row == 1, middle, jnp.where(row == 2, low, 0.0)))
    return parts.astype(BF16)


def total_of(ref, i):
    parts = ref[i, ref.shape[1] - PAD :, :].astype(F32)
    return parts[0:1, :] + parts[1:2, :] + parts[2:3, :]


def states_kernel(decay_ref, keys_ref, values_ref, out_ref):
    heads, count = decay_ref.shape
    pieces = out_ref.shape[0] // heads
    rows = HD // pieces
    within = within_rows(decay_ref[...])
    total = within[:, count - 1 : count]
    coef = jnp.exp(total - within)
    for h in range(heads):
        cols = slice(h * HD, (h + 1) * HD)
        keys_t = keys_ref[:, cols].astype(F32).T * coef[h : h + 1, :]
        state = dot(keys_t.astype(BF16), values_ref[:, cols], 1, 0).astype(BF16)
        parts = parts_of(total[h : h + 1, :])
        for j in range(pieces):
            out_ref[h * pieces + j, :rows, :] = state[rows * j : rows * (j + 1), :]
            out_ref[h * pieces + j, rows:, :] = parts


def group_kernel(group_ref, out_ref):
    rows = group_ref.shape[1] - PAD
    state = jnp.zeros((rows, HD), F32)
    total = jnp.zeros((1, HD), F32)
    for i in range(group_ref.shape[0]):
        step = total_of(group_ref, i)
        state = jnp.exp(step) * state + group_ref[i, :rows, :].astype(F32)
        total = total + step
    state = state.astype(BF16)
    parts = parts_of(total)
    for j in range(out_ref.shape[0]):
        out_ref[j, :rows, :] = state
        out_ref[j, rows:, :] = parts


def prior_kernel(place_ref, totals_ref, group_ref, out_ref):
    rows = out_ref.shape[1]
    place = place_ref[0]
    state = jnp.zeros((rows, HD), F32)
    for i in range(totals_ref.shape[0]):
        later = jnp.exp(total_of(totals_ref, i)) * state + totals_ref[i, :rows, :].astype(F32)
        state = jnp.where(i < place, later, state)
    for i in range(group_ref.shape[0]):
        out_ref[i] = state.astype(BF16)
        state = jnp.exp(total_of(group_ref, i)) * state + group_ref[i, :rows, :].astype(F32)


def local_kernel(decay_ref, queries_ref, keys_ref, values_ref, out_ref):
    heads, count = decay_ref.shape
    rows = within_rows(decay_ref[...])
    cols = within_cols(decay_ref[...])
    causal = lax.broadcasted_iota(jnp.int32, (count, count), 0) >= lax.broadcasted_iota(
        jnp.int32, (count, count), 1
    )
    for h in range(heads):
        part = slice(h * HD, (h + 1) * HD)
        scores = dot(queries_ref[:, part], keys_ref[:, part], 1, 1)
        gaps = cols[:, h : h + 1] - rows[h : h + 1, :]
        decay = jnp.exp(jnp.where(causal, gaps, -jnp.inf))
        weights = (scores * decay).astype(BF16)
        out_ref[:, part] = dot(weights, values_ref[:, part], 1, 0)


def norm_kernel(decay_ref, queries_ref, local_ref, prior_ref, out_ref):
    heads = decay_ref.shape[0]
    scale = jnp.exp(within_cols(decay_ref[...]))
    place = lax.broadcasted_iota(jnp.int32, (HD, HD), 1)
    source = lax.broadcasted_iota(jnp.int32, (HD, HD), 0)
    quarter = HD // 8
    wanted = (place // 4 % 2) * (4 * quarter) + (place // 8) * 4 + place % 4
    reorder = (source == wanted).astype(BF16)
    for h in range(heads):
        part = slice(h * HD, (h + 1) * HD)
        carried = dot(queries_ref[:, part], prior_ref[h], 1, 0) * scale[:, h : h + 1]
        combined = local_ref[:, part] + carried
        square = jnp.mean(combined * combined, axis=-1, keepdims=True)
        normed = (combined * lax.rsqrt(square + 1e-05)).astype(BF16)
        out_ref[:, part] = dot(normed, reorder, 1, 0).astype(BF16)


def project_kernel(normed_ref, weight_ref, out_ref, rows_ref, sems):
    heads = weight_ref.shape[1]

    def copy(h):
        return pltpu.make_async_copy(weight_ref.at[:, h], rows_ref.at[h], sems.at[h])

    for h in range(heads):
        copy(h).start()
    acc = jnp.zeros(out_ref.shape, F32)
    for h in range(0, heads, 2):
        copy(h).wait()
        copy(h + 1).wait()
        rows = rows_ref[h : h + 2].reshape(2 * HD, out_ref.shape[1])
        acc = acc + dot(normed_ref[:, h * HD : (h + 2) * HD], rows, 1, 0)
    out_ref[...] = acc.astype(BF16)


def swap(x, within):
    return lax.all_to_all(
        x, ("seq", "head"), split_axis=0, concat_axis=0, axis_index_groups=within, tiled=True
    )


def shape(*dims, kind=F32):
    return jax.ShapeDtypeStruct(dims, kind)


def mix(queries, keys, values, log_decay, out_weight):
    count, width = queries.shape
    heads = log_decay.shape[1]
    groups = lax.axis_size("seq")
    members = lax.axis_size("head")
    decay_t = log_decay.T
    size = NEAR
    rows = HD * heads // size
    devices = groups * members
    near = [list(range(i, i + size)) for i in range(0, devices, size)]
    far = [list(range(i, devices, size)) for i in range(size)]

    weight_rows = out_weight.shape[0]
    spread = jnp.broadcast_to(out_weight[None], (groups, weight_rows, width))
    spread = lax.all_to_all(spread, "seq", split_axis=0, concat_axis=0, tiled=True)
    spread = spread.reshape(groups * weight_rows, width)
    weight = lax.all_gather(spread, "head", axis=0, tiled=True)

    own = pl.pallas_call(
        states_kernel, out_shape=shape(size, rows + PAD, HD, kind=BF16), compiler_params=VMEM
    )(decay_t, keys, values)
    group = swap(own, near)
    local_part = pl.pallas_call(
        local_kernel, out_shape=shape(count, width), compiler_params=VMEM
    )(decay_t, queries, keys, values)
    totals = pl.pallas_call(
        group_kernel,
        out_shape=shape(len(far[0]), rows + PAD, HD, kind=BF16),
        compiler_params=VMEM,
    )(group)
    totals = swap(totals, far)
    place = (lax.axis_index("seq") * members + lax.axis_index("head")) // size
    vmem = pl.BlockSpec(memory_space=pltpu.VMEM)
    prior = pl.pallas_call(
        prior_kernel,
        in_specs=[pl.BlockSpec(memory_space=pltpu.SMEM), vmem, vmem],
        out_specs=vmem,
        out_shape=shape(size, rows, HD, kind=BF16),
        compiler_params=VMEM,
    )(place.reshape(1), totals, group)
    prior = swap(prior, near).reshape(heads, HD, HD)
    normed = pl.pallas_call(
        norm_kernel, out_shape=shape(count, width, kind=BF16), compiler_params=VMEM
    )(decay_t, queries, local_part, prior)
    runs = 2 * weight_rows
    weight = weight.reshape(members, groups // 2, runs, width)
    weight = pltpu.with_memory_space_constraint(weight, pltpu.HBM)
    return pl.pallas_call(
        project_kernel,
        out_shape=shape(count, width, kind=BF16),
        in_specs=[vmem, pl.BlockSpec(memory_space=pltpu.HBM)],
        out_specs=vmem,
        scratch_shapes=[
            pltpu.VMEM((heads, members, runs, width), BF16),
            pltpu.SemaphoreType.DMA((heads,)),
        ],
        compiler_params=VMEM,
    )(normed, weight)


def solution(mesh):
    placed = P(("seq", "head"), None)
    return jax.shard_map(mix, mesh=mesh, in_specs=(placed,) * 5, out_specs=placed, check_vma=False)
```

```python
import jax
import jax.numpy as jnp
from jax import lax
from jax.experimental import pallas as pl
from jax.experimental.pallas import tpu as pltpu
from jax.sharding import PartitionSpec as P

HD = 128
PAD = 8
NEAR = 16
BF16 = jnp.bfloat16
F32 = jnp.float32
VMEM = pltpu.CompilerParams(vmem_limit_bytes=40 * 1024 * 1024)


def ones_below(rows):
    return (
        lax.broadcasted_iota(jnp.int32, (rows, rows), 0)
        >= lax.broadcasted_iota(jnp.int32, (rows, rows), 1)
    ).astype(BF16)


def dot(a, b, ca, cb):
    return lax.dot_general(a, b, (((ca,), (cb,)), ((), ())), preferred_element_type=F32)


def within_rows(decay_t):
    return dot(decay_t, ones_below(decay_t.shape[1]), 1, 1)


def within_cols(decay_t):
    return dot(ones_below(decay_t.shape[1]), decay_t, 1, 1)


def parts_of(total):
    row = lax.broadcasted_iota(jnp.int32, (PAD, HD), 0)
    whole = jnp.broadcast_to(total, (PAD, HD))
    high = whole.astype(BF16).astype(F32)
    middle = (whole - high).astype(BF16).astype(F32)
    low = whole - high - middle
    parts = jnp.where(row == 0, high, jnp.where(row == 1, middle, jnp.where(row == 2, low, 0.0)))
    return parts.astype(BF16)


def total_of(ref, i):
    parts = ref[i, ref.shape[1] - PAD :, :].astype(F32)
    return parts[0:1, :] + parts[1:2, :] + parts[2:3, :]


def pack_kernel(core_ref, decay_ref, queries_ref, keys_ref, values_ref, own_ref, other_ref):
    first = core_ref[0] == 0
    half = (own_ref.shape[0] - 1) // 3
    for n, ref in enumerate((keys_ref, values_ref, queries_ref)):
        for h in range(half):
            low = ref[:, h * HD : (h + 1) * HD]
            high = ref[:, (half + h) * HD : (half + h + 1) * HD]
            own_ref[n * half + h] = jnp.where(first, low, high)
            other_ref[n * half + h] = jnp.where(first, high, low)
    low = decay_ref[:half, :].astype(F32)
    high = decay_ref[half:, :].astype(F32)
    rest = jnp.zeros((HD - half, HD), F32)
    kept = jnp.concatenate([jnp.where(first, low, high), rest], axis=0)
    sent = jnp.concatenate([jnp.where(first, high, low), rest], axis=0)
    own_ref[3 * half] = kept.astype(BF16)
    other_ref[3 * half] = sent.astype(BF16)


def both(first, own_ref, other_ref, i):
    own, other = own_ref[i], other_ref[i]
    return jnp.where(first, own, other), jnp.where(first, other, own)


def tokens(first, own_ref, other_ref, i):
    return jnp.concatenate(both(first, own_ref, other_ref, i), axis=0)


def decays(first, own_ref, other_ref):
    half = (own_ref.shape[0] - 1) // 3
    early, late = both(first, own_ref, other_ref, 3 * half)
    return jnp.concatenate([early[:half, :], late[:half, :]], axis=1)


def states_kernel(core_ref, own_ref, other_ref, out_ref):
    first = core_ref[0] == 0
    heads = (own_ref.shape[0] - 1) // 3
    pieces = out_ref.shape[0] // heads
    rows = HD // pieces
    decay_t = decays(first, own_ref, other_ref)
    count = decay_t.shape[1]
    within = within_rows(decay_t)
    total = within[:, count - 1 : count]
    coef = jnp.exp(total - within)
    for h in range(heads):
        keys_t = tokens(first, own_ref, other_ref, h).astype(F32).T * coef[h : h + 1, :]
        values = tokens(first, own_ref, other_ref, heads + h)
        state = dot(keys_t.astype(BF16), values, 1, 0).astype(BF16)
        parts = parts_of(total[h : h + 1, :])
        for j in range(pieces):
            out_ref[h * pieces + j, :rows, :] = state[rows * j : rows * (j + 1), :]
            out_ref[h * pieces + j, rows:, :] = parts


def group_kernel(group_ref, out_ref):
    rows = group_ref.shape[1] - PAD
    state = jnp.zeros((rows, HD), F32)
    total = jnp.zeros((1, HD), F32)
    for i in range(group_ref.shape[0]):
        step = total_of(group_ref, i)
        state = jnp.exp(step) * state + group_ref[i, :rows, :].astype(F32)
        total = total + step
    state = state.astype(BF16)
    parts = parts_of(total)
    for j in range(out_ref.shape[0]):
        out_ref[j, :rows, :] = state
        out_ref[j, rows:, :] = parts


def prior_kernel(place_ref, totals_ref, group_ref, out_ref):
    rows = out_ref.shape[1]
    place = place_ref[0]
    state = jnp.zeros((rows, HD), F32)
    for i in range(totals_ref.shape[0]):
        later = jnp.exp(total_of(totals_ref, i)) * state + totals_ref[i, :rows, :].astype(F32)
        state = jnp.where(i < place, later, state)
    for i in range(group_ref.shape[0]):
        out_ref[i] = state.astype(BF16)
        state = jnp.exp(total_of(group_ref, i)) * state + group_ref[i, :rows, :].astype(F32)


def local_kernel(core_ref, own_ref, other_ref, out_ref):
    first = core_ref[0] == 0
    heads, count, _ = out_ref.shape
    decay_t = decays(first, own_ref, other_ref)
    rows = within_rows(decay_t)
    cols = within_cols(decay_t)
    causal = lax.broadcasted_iota(jnp.int32, (count, count), 0) >= lax.broadcasted_iota(
        jnp.int32, (count, count), 1
    )
    for h in range(heads):
        keys = tokens(first, own_ref, other_ref, h)
        values = tokens(first, own_ref, other_ref, heads + h)
        queries = tokens(first, own_ref, other_ref, 2 * heads + h)
        scores = dot(queries, keys, 1, 1)
        gaps = cols[:, h : h + 1] - rows[h : h + 1, :]
        decay = jnp.exp(jnp.where(causal, gaps, -jnp.inf))
        weights = (scores * decay).astype(BF16)
        out_ref[h] = dot(weights, values, 1, 0)


def norm_kernel(core_ref, own_ref, other_ref, local_ref, prior_ref, keep_ref, send_ref):
    first = core_ref[0] == 0
    heads = local_ref.shape[0]
    count = keep_ref.shape[1]
    scale = jnp.exp(within_cols(decays(first, own_ref, other_ref)))
    place = lax.broadcasted_iota(jnp.int32, (HD, HD), 1)
    source = lax.broadcasted_iota(jnp.int32, (HD, HD), 0)
    wanted = (place // 4 % 2) * (HD // 2) + (place // 8) * 4 + place % 4
    reorder = (source == wanted).astype(BF16)
    for h in range(heads):
        queries = tokens(first, own_ref, other_ref, 2 * heads + h)
        carried = dot(queries, prior_ref[h], 1, 0) * scale[:, h : h + 1]
        combined = local_ref[h] + carried
        square = jnp.mean(combined * combined, axis=-1, keepdims=True)
        normed = (combined * lax.rsqrt(square + 1e-05)).astype(BF16)
        normed = dot(normed, reorder, 1, 0).astype(BF16)
        keep_ref[h] = jnp.where(first, normed[:count], normed[count:])
        send_ref[h] = jnp.where(first, normed[count:], normed[:count])


def project_kernel(core_ref, kept_ref, got_ref, weight_ref, out_ref, rows_ref, sems):
    first = core_ref[0] == 0
    heads = weight_ref.shape[1]
    half = heads // 2

    def copy(h):
        return pltpu.make_async_copy(weight_ref.at[:, h], rows_ref.at[h], sems.at[h])

    def normed(h):
        low, high = both(first, kept_ref, got_ref, h % half)
        return low if h < half else high

    for h in range(heads):
        copy(h).start()
    acc = jnp.zeros(out_ref.shape, F32)
    for h in range(0, heads, 2):
        copy(h).wait()
        copy(h + 1).wait()
        rows = rows_ref[h : h + 2].reshape(2 * HD, out_ref.shape[1])
        acc = acc + dot(jnp.concatenate([normed(h), normed(h + 1)], axis=1), rows, 1, 0)
    out_ref[...] = acc.astype(BF16)


def swap(x, within):
    return lax.all_to_all(
        x, ("seq", "head"), split_axis=0, concat_axis=0, axis_index_groups=within, tiled=True
    )


def shape(*dims, kind=F32):
    return jax.ShapeDtypeStruct(dims, kind)


def call(kernel, out, *args, **options):
    vmem = pl.BlockSpec(memory_space=pltpu.VMEM)
    smem = pl.BlockSpec(memory_space=pltpu.SMEM)
    return pl.pallas_call(
        kernel,
        out_shape=out,
        in_specs=[smem] + [vmem] * (len(args) - 1),
        out_specs=jax.tree.map(lambda _: vmem, out),
        compiler_params=VMEM,
        **options,
    )(*args)


def mix(queries, keys, values, log_decay, out_weight):
    count, width = queries.shape
    heads = log_decay.shape[1]
    half = heads // 2
    groups = lax.axis_size("seq")
    members = lax.axis_size("head")
    decay_t = log_decay.T
    devices = groups * members
    size = 2 * NEAR
    rows = HD * half // NEAR
    near = [list(range(i + c, i + size, 2)) for i in range(0, devices, size) for c in range(2)]
    far = [list(range(i, devices, size)) for i in range(size)]
    partner = [(i, i ^ 1) for i in range(members)]
    core = (lax.axis_index("head") & 1).reshape(1)
    place = (lax.axis_index("seq") // (size // members)).reshape(1)

    weight_rows = out_weight.shape[0]
    spread = jnp.broadcast_to(out_weight[None], (groups, weight_rows, width))
    spread = lax.all_to_all(spread, "seq", split_axis=0, concat_axis=0, tiled=True)
    spread = spread.reshape(groups * weight_rows, width)
    weight = lax.all_gather(spread, "head", axis=0, tiled=True)

    pair = shape(3 * half + 1, count, HD, kind=BF16)
    own, other = call(pack_kernel, (pair, pair), core, decay_t, queries, keys, values)
    other = lax.ppermute(other, "head", partner)
    states = call(states_kernel, shape(NEAR, rows + PAD, HD, kind=BF16), core, own, other)
    local_part = call(local_kernel, shape(half, 2 * count, HD), core, own, other)
    group = swap(states, near)
    totals = pl.pallas_call(
        group_kernel,
        out_shape=shape(len(far[0]), rows + PAD, HD, kind=BF16),
        compiler_params=VMEM,
    )(group)
    totals = swap(totals, far)
    prior = call(prior_kernel, shape(NEAR, rows, HD, kind=BF16), place, totals, group)
    prior = swap(prior, near).reshape(half, HD, HD)
    normed = shape(half, count, HD, kind=BF16)
    kept, sent = call(norm_kernel, (normed, normed), core, own, other, local_part, prior)
    got = lax.ppermute(sent, "head", partner)
    weight = weight.reshape(members, groups // 2, 2 * weight_rows, width)
    weight = pltpu.with_memory_space_constraint(weight, pltpu.HBM)
    vmem = pl.BlockSpec(memory_space=pltpu.VMEM)
    return pl.pallas_call(
        project_kernel,
        out_shape=shape(count, width, kind=BF16),
        in_specs=[
            pl.BlockSpec(memory_space=pltpu.SMEM),
            vmem,
            vmem,
            pl.BlockSpec(memory_space=pltpu.HBM),
        ],
        out_specs=vmem,
        scratch_shapes=[
            pltpu.VMEM((heads, members, 2 * weight_rows, width), BF16),
            pltpu.SemaphoreType.DMA((heads,)),
        ],
        compiler_params=VMEM,
    )(core, kept, got, weight)


def solution(mesh):
    placed = P(("seq", "head"), None)
    return jax.shard_map(mix, mesh=mesh, in_specs=(placed,) * 5, out_specs=placed, check_vma=False)
```

```python
import jax
import jax.numpy as jnp
from jax import lax
from jax.experimental import pallas as pl
from jax.experimental.pallas import tpu as pltpu
from jax.sharding import PartitionSpec as P

HD = 128
PAD = 8
NEAR = 16
RUN = 4
BF16 = jnp.bfloat16
F32 = jnp.float32
VMEM = pltpu.CompilerParams(vmem_limit_bytes=12 * 1024 * 1024)
LARGE = pltpu.CompilerParams(vmem_limit_bytes=20 * 1024 * 1024)


def ones_below(rows):
    return (
        lax.broadcasted_iota(jnp.int32, (rows, rows), 0)
        >= lax.broadcasted_iota(jnp.int32, (rows, rows), 1)
    ).astype(BF16)


def dot(a, b, ca, cb):
    return lax.dot_general(a, b, (((ca,), (cb,)), ((), ())), preferred_element_type=F32)


def within_rows(decay_t):
    return dot(decay_t, ones_below(decay_t.shape[1]), 1, 1)


def within_cols(decay_t):
    return dot(ones_below(decay_t.shape[1]), decay_t, 1, 1)


def parts_of(total):
    row = lax.broadcasted_iota(jnp.int32, (PAD, HD), 0)
    whole = jnp.broadcast_to(total, (PAD, HD))
    high = whole.astype(BF16).astype(F32)
    middle = (whole - high).astype(BF16).astype(F32)
    low = whole - high - middle
    parts = jnp.where(row == 0, high, jnp.where(row == 1, middle, jnp.where(row == 2, low, 0.0)))
    return parts.astype(BF16)


def total_of(ref, i):
    parts = ref[i, ref.shape[1] - PAD :, :].astype(F32)
    return parts[0:1, :] + parts[1:2, :] + parts[2:3, :]


def spread_kernel(weight_ref, out_ref):
    for i in range(out_ref.shape[0]):
        out_ref[i] = weight_ref[...]


def merge_kernel(in_ref, out_ref):
    for i in range(0, in_ref.shape[0], 2):
        pair = jnp.concatenate([in_ref[i], in_ref[i + 1]], axis=0)
        out_ref[4 * i : 4 * i + 8, :] = pair


def pack_kernel(core_ref, decay_ref, queries_ref, keys_ref, values_ref, own_ref, other_ref):
    first = core_ref[0] == 0
    half = (own_ref.shape[0] - 1) // 3
    for n, ref in enumerate((keys_ref, values_ref, queries_ref)):
        for h in range(half):
            low = ref[:, h * HD : (h + 1) * HD]
            high = ref[:, (half + h) * HD : (half + h + 1) * HD]
            own_ref[n * half + h] = jnp.where(first, low, high)
            other_ref[n * half + h] = jnp.where(first, high, low)
    low = decay_ref[:half, :].astype(F32)
    high = decay_ref[half:, :].astype(F32)
    rest = jnp.zeros((HD - half, HD), F32)
    kept = jnp.concatenate([jnp.where(first, low, high), rest], axis=0)
    sent = jnp.concatenate([jnp.where(first, high, low), rest], axis=0)
    own_ref[3 * half] = kept.astype(BF16)
    other_ref[3 * half] = sent.astype(BF16)


def both(first, own_ref, other_ref, i):
    own, other = own_ref[i], other_ref[i]
    return jnp.where(first, own, other), jnp.where(first, other, own)


def tokens(first, own_ref, other_ref, i):
    return jnp.concatenate(both(first, own_ref, other_ref, i), axis=0)


def decays(first, own_ref, other_ref):
    half = (own_ref.shape[0] - 1) // 3
    early, late = both(first, own_ref, other_ref, 3 * half)
    return jnp.concatenate([early[:half, :], late[:half, :]], axis=1)


def states_kernel(core_ref, own_ref, other_ref, out_ref):
    first = core_ref[0] == 0
    heads = (own_ref.shape[0] - 1) // 3
    pieces = out_ref.shape[0] // heads
    rows = HD // pieces
    decay_t = decays(first, own_ref, other_ref)
    count = decay_t.shape[1]
    within = within_rows(decay_t)
    total = within[:, count - 1 : count]
    coef = jnp.exp(total - within)
    for h in range(heads):
        keys_t = tokens(first, own_ref, other_ref, h).astype(F32).T * coef[h : h + 1, :]
        values = tokens(first, own_ref, other_ref, heads + h)
        state = dot(keys_t.astype(BF16), values, 1, 0).astype(BF16)
        parts = parts_of(total[h : h + 1, :])
        for j in range(pieces):
            out_ref[h * pieces + j, :rows, :] = state[rows * j : rows * (j + 1), :]
            out_ref[h * pieces + j, rows:, :] = parts


def group_kernel(group_ref, out_ref):
    rows = group_ref.shape[1] - PAD
    state = jnp.zeros((rows, HD), F32)
    total = jnp.zeros((1, HD), F32)
    for i in range(group_ref.shape[0]):
        step = total_of(group_ref, i)
        state = jnp.exp(step) * state + group_ref[i, :rows, :].astype(F32)
        total = total + step
    state = state.astype(BF16)
    parts = parts_of(total)
    for j in range(out_ref.shape[0]):
        out_ref[j, :rows, :] = state
        out_ref[j, rows:, :] = parts


def prior_kernel(place_ref, totals_ref, group_ref, out_ref):
    rows = out_ref.shape[1]
    place = place_ref[0]
    state = jnp.zeros((rows, HD), F32)
    for i in range(totals_ref.shape[0]):
        later = jnp.exp(total_of(totals_ref, i)) * state + totals_ref[i, :rows, :].astype(F32)
        state = jnp.where(i < place, later, state)
    for i in range(group_ref.shape[0]):
        out_ref[i] = state.astype(BF16)
        state = jnp.exp(total_of(group_ref, i)) * state + group_ref[i, :rows, :].astype(F32)


def local_kernel(core_ref, own_ref, other_ref, out_ref):
    first = core_ref[0] == 0
    heads, count, _ = out_ref.shape
    decay_t = decays(first, own_ref, other_ref)
    rows = within_rows(decay_t)
    cols = within_cols(decay_t)
    causal = lax.broadcasted_iota(jnp.int32, (count, count), 0) >= lax.broadcasted_iota(
        jnp.int32, (count, count), 1
    )
    for h in range(heads):
        keys = tokens(first, own_ref, other_ref, h)
        values = tokens(first, own_ref, other_ref, heads + h)
        queries = tokens(first, own_ref, other_ref, 2 * heads + h)
        scores = dot(queries, keys, 1, 1)
        gaps = cols[:, h : h + 1] - rows[h : h + 1, :]
        decay = jnp.exp(jnp.where(causal, gaps, -jnp.inf))
        weights = (scores * decay).astype(BF16)
        out_ref[h] = dot(weights, values, 1, 0)


def norm_kernel(core_ref, own_ref, other_ref, local_ref, prior_ref, keep_ref, send_ref):
    first = core_ref[0] == 0
    heads = local_ref.shape[0]
    count = keep_ref.shape[1]
    scale = jnp.exp(within_cols(decays(first, own_ref, other_ref)))
    place = lax.broadcasted_iota(jnp.int32, (HD, HD), 1)
    source = lax.broadcasted_iota(jnp.int32, (HD, HD), 0)
    wanted = (place // 4 % 2) * (HD // 2) + (place // 8) * 4 + place % 4
    reorder = (source == wanted).astype(BF16)
    for h in range(heads):
        queries = tokens(first, own_ref, other_ref, 2 * heads + h)
        carried = dot(queries, prior_ref[h], 1, 0) * scale[:, h : h + 1]
        combined = local_ref[h] + carried
        square = jnp.mean(combined * combined, axis=-1, keepdims=True)
        normed = (combined * lax.rsqrt(square + 1e-05)).astype(BF16)
        normed = dot(normed, reorder, 1, 0).astype(BF16)
        keep_ref[h] = jnp.where(first, normed[:count], normed[count:])
        send_ref[h] = jnp.where(first, normed[count:], normed[:count])


def project_kernel(core_ref, kept_ref, got_ref, weight_ref, out_ref, rows_ref, sems):
    first = core_ref[0] == 0
    heads = weight_ref.shape[1]
    half = heads // 2

    def copy(h):
        return pltpu.make_async_copy(weight_ref.at[:, h], rows_ref.at[h], sems.at[h])

    def normed(h):
        low, high = both(first, kept_ref, got_ref, h % half)
        return low if h < half else high

    for h in range(heads):
        copy(h).start()
    acc = jnp.zeros(out_ref.shape, F32)
    for h in range(0, heads, RUN):
        run = range(h, h + RUN)
        for i in run:
            copy(i).wait()
        rows = rows_ref[h : h + RUN].reshape(RUN * HD, out_ref.shape[1])
        acc = acc + dot(jnp.concatenate([normed(i) for i in run], axis=1), rows, 1, 0)
    out_ref[...] = acc.astype(BF16)


def swap(x, within):
    return lax.all_to_all(
        x, ("seq", "head"), split_axis=0, concat_axis=0, axis_index_groups=within, tiled=True
    )


def shape(*dims, kind=F32):
    return jax.ShapeDtypeStruct(dims, kind)


def call(kernel, out, *args, **options):
    vmem = pl.BlockSpec(memory_space=pltpu.VMEM)
    smem = pl.BlockSpec(memory_space=pltpu.SMEM)
    return pl.pallas_call(
        kernel,
        out_shape=out,
        in_specs=[smem] + [vmem] * (len(args) - 1),
        out_specs=jax.tree.map(lambda _: vmem, out),
        compiler_params=VMEM,
        **options,
    )(*args)


def mix(queries, keys, values, log_decay, out_weight):
    count, width = queries.shape
    heads = log_decay.shape[1]
    half = heads // 2
    groups = lax.axis_size("seq")
    members = lax.axis_size("head")
    decay_t = log_decay.T
    devices = groups * members
    size = 2 * NEAR
    rows = HD * half // NEAR
    near = [list(range(i + c, i + size, 2)) for i in range(0, devices, size) for c in range(2)]
    far = [list(range(i, devices, size)) for i in range(size)]
    partner = [(i, i ^ 1) for i in range(members)]
    core = (lax.axis_index("head") & 1).reshape(1)
    place = (lax.axis_index("seq") // (size // members)).reshape(1)

    weight_rows = out_weight.shape[0]
    spread = pl.pallas_call(
        spread_kernel, out_shape=shape(groups, weight_rows, width, kind=BF16), compiler_params=VMEM
    )(out_weight)
    spread = lax.all_to_all(spread, "seq", split_axis=0, concat_axis=0, tiled=True)
    spread = pl.pallas_call(
        merge_kernel, out_shape=shape(groups * weight_rows, width, kind=BF16), compiler_params=VMEM
    )(spread)
    weight = lax.all_gather(spread, "head", axis=0, tiled=True)

    pair = shape(3 * half + 1, count, HD, kind=BF16)
    own, other = call(pack_kernel, (pair, pair), core, decay_t, queries, keys, values)
    other = lax.ppermute(other, "head", partner)
    states = call(states_kernel, shape(NEAR, rows + PAD, HD, kind=BF16), core, own, other)
    local_part = call(local_kernel, shape(half, 2 * count, HD), core, own, other)
    group = swap(states, near)
    totals = pl.pallas_call(
        group_kernel,
        out_shape=shape(len(far[0]), rows + PAD, HD, kind=BF16),
        compiler_params=VMEM,
    )(group)
    totals = swap(totals, far)
    prior = call(prior_kernel, shape(NEAR, rows, HD, kind=BF16), place, totals, group)
    prior = swap(prior, near).reshape(half, HD, HD)
    normed = shape(half, count, HD, kind=BF16)
    kept, sent = call(norm_kernel, (normed, normed), core, own, other, local_part, prior)
    got = lax.ppermute(sent, "head", partner)
    weight = weight.reshape(members, groups // 2, 2 * weight_rows, width)
    weight = pltpu.with_memory_space_constraint(weight, pltpu.HBM)
    vmem = pl.BlockSpec(memory_space=pltpu.VMEM)
    return pl.pallas_call(
        project_kernel,
        out_shape=shape(count, width, kind=BF16),
        in_specs=[
            pl.BlockSpec(memory_space=pltpu.SMEM),
            vmem,
            vmem,
            pl.BlockSpec(memory_space=pltpu.HBM),
        ],
        out_specs=vmem,
        scratch_shapes=[
            pltpu.VMEM((heads, members, 2 * weight_rows, width), BF16),
            pltpu.SemaphoreType.DMA((heads,)),
        ],
        compiler_params=LARGE,
    )(core, kept, got, weight)


def solution(mesh):
    placed = P(("seq", "head"), None)
    return jax.shard_map(mix, mesh=mesh, in_specs=(placed,) * 5, out_specs=placed, check_vma=False)
```

```python
import jax
import jax.numpy as jnp
from jax import lax
from jax.experimental import pallas as pl
from jax.experimental.pallas import tpu as pltpu
from jax.sharding import PartitionSpec as P

HD = 128
PAD = 8
NEAR = 16
RUN = 2
ROW = 8
BF16 = jnp.bfloat16
F32 = jnp.float32
VMEM = pltpu.CompilerParams(vmem_limit_bytes=12 * 1024 * 1024)
LARGE = pltpu.CompilerParams(vmem_limit_bytes=20 * 1024 * 1024)


def ones_below(rows):
    return (
        lax.broadcasted_iota(jnp.int32, (rows, rows), 0)
        >= lax.broadcasted_iota(jnp.int32, (rows, rows), 1)
    ).astype(BF16)


def dot(a, b, ca, cb):
    return lax.dot_general(a, b, (((ca,), (cb,)), ((), ())), preferred_element_type=F32)


def within_rows(decay_t):
    return dot(decay_t, ones_below(decay_t.shape[1]), 1, 1)


def within_cols(decay_t):
    return dot(ones_below(decay_t.shape[1]), decay_t, 1, 1)


def parts_of(total):
    row = lax.broadcasted_iota(jnp.int32, (PAD, HD), 0)
    whole = jnp.broadcast_to(total, (PAD, HD))
    high = whole.astype(BF16).astype(F32)
    middle = (whole - high).astype(BF16).astype(F32)
    low = whole - high - middle
    parts = jnp.where(row == 0, high, jnp.where(row == 1, middle, jnp.where(row == 2, low, 0.0)))
    return parts.astype(BF16)


def total_of(ref, i):
    parts = ref[i, ref.shape[1] - PAD :, :].astype(F32)
    return parts[0:1, :] + parts[1:2, :] + parts[2:3, :]


def spread_kernel(weight_ref, out_ref):
    for i in range(out_ref.shape[0]):
        out_ref[i] = weight_ref[...]


def merge_kernel(in_ref, out_ref):
    for i in range(0, in_ref.shape[0], 2):
        pair = jnp.concatenate([in_ref[i], in_ref[i + 1]], axis=0)
        out_ref[4 * i : 4 * i + 8, :] = pair


def pack_kernel(core_ref, decay_ref, queries_ref, keys_ref, values_ref, own_ref, other_ref):
    first = core_ref[0] == 0
    half = (own_ref.shape[0] - 1) // 3
    for n, ref in enumerate((keys_ref, values_ref, queries_ref)):
        for h in range(half):
            low = ref[:, h * HD : (h + 1) * HD]
            high = ref[:, (half + h) * HD : (half + h + 1) * HD]
            own_ref[n * half + h] = jnp.where(first, low, high)
            other_ref[n * half + h] = jnp.where(first, high, low)
    low = decay_ref[:half, :].astype(F32)
    high = decay_ref[half:, :].astype(F32)
    rest = jnp.zeros((HD - half, HD), F32)
    kept = jnp.concatenate([jnp.where(first, low, high), rest], axis=0)
    sent = jnp.concatenate([jnp.where(first, high, low), rest], axis=0)
    own_ref[3 * half] = kept.astype(BF16)
    other_ref[3 * half] = sent.astype(BF16)


def both(first, own_ref, other_ref, i):
    own, other = own_ref[i], other_ref[i]
    return jnp.where(first, own, other), jnp.where(first, other, own)


def tokens(first, own_ref, other_ref, i):
    return jnp.concatenate(both(first, own_ref, other_ref, i), axis=0)


def decays(first, own_ref, other_ref):
    half = (own_ref.shape[0] - 1) // 3
    early, late = both(first, own_ref, other_ref, 3 * half)
    return jnp.concatenate([early[:half, :], late[:half, :]], axis=1)


def states_kernel(core_ref, own_ref, other_ref, out_ref):
    first = core_ref[0] == 0
    heads = (own_ref.shape[0] - 1) // 3
    pieces = out_ref.shape[0] // heads
    rows = HD // pieces
    decay_t = decays(first, own_ref, other_ref)
    count = decay_t.shape[1]
    within = within_rows(decay_t)
    total = within[:, count - 1 : count]
    coef = jnp.exp(total - within)
    for h in range(heads):
        keys_t = tokens(first, own_ref, other_ref, h).astype(F32).T * coef[h : h + 1, :]
        values = tokens(first, own_ref, other_ref, heads + h)
        state = dot(keys_t.astype(BF16), values, 1, 0).astype(BF16)
        parts = parts_of(total[h : h + 1, :])
        for j in range(pieces):
            out_ref[h * pieces + j, :rows, :] = state[rows * j : rows * (j + 1), :]
            out_ref[h * pieces + j, rows:, :] = parts


def group_kernel(group_ref, out_ref):
    rows = group_ref.shape[1] - PAD
    state = jnp.zeros((rows, HD), F32)
    total = jnp.zeros((1, HD), F32)
    for i in range(group_ref.shape[0]):
        step = total_of(group_ref, i)
        state = jnp.exp(step) * state + group_ref[i, :rows, :].astype(F32)
        total = total + step
    state = state.astype(BF16)
    parts = parts_of(total)
    for j in range(out_ref.shape[0]):
        out_ref[j, :rows, :] = state
        out_ref[j, rows:, :] = parts


def prior_kernel(place_ref, totals_ref, group_ref, out_ref):
    rows = out_ref.shape[1]
    place = place_ref[0]
    state = jnp.zeros((rows, HD), F32)
    for i in range(totals_ref.shape[0]):
        later = jnp.exp(total_of(totals_ref, i)) * state + totals_ref[i, :rows, :].astype(F32)
        state = jnp.where(i < place, later, state)
    for i in range(group_ref.shape[0]):
        out_ref[i] = state.astype(BF16)
        state = jnp.exp(total_of(group_ref, i)) * state + group_ref[i, :rows, :].astype(F32)


def local_kernel(core_ref, own_ref, other_ref, out_ref):
    first = core_ref[0] == 0
    heads, count, _ = out_ref.shape
    decay_t = decays(first, own_ref, other_ref)
    rows = within_rows(decay_t)
    cols = within_cols(decay_t)
    causal = lax.broadcasted_iota(jnp.int32, (count, count), 0) >= lax.broadcasted_iota(
        jnp.int32, (count, count), 1
    )
    for h in range(heads):
        keys = tokens(first, own_ref, other_ref, h)
        values = tokens(first, own_ref, other_ref, heads + h)
        queries = tokens(first, own_ref, other_ref, 2 * heads + h)
        scores = dot(queries, keys, 1, 1)
        gaps = cols[:, h : h + 1] - rows[h : h + 1, :]
        decay = jnp.exp(jnp.where(causal, gaps, -jnp.inf))
        weights = (scores * decay).astype(BF16)
        out_ref[h] = dot(weights, values, 1, 0)


def norm_kernel(core_ref, own_ref, other_ref, local_ref, prior_ref, keep_ref, send_ref):
    first = core_ref[0] == 0
    heads = local_ref.shape[0]
    count = keep_ref.shape[1]
    scale = jnp.exp(within_cols(decays(first, own_ref, other_ref)))
    place = lax.broadcasted_iota(jnp.int32, (HD, HD), 1)
    source = lax.broadcasted_iota(jnp.int32, (HD, HD), 0)
    wanted = (place // 64) * 64 + (place % 32 // 4) * 8 + (place // 32 % 2) * 4 + place % 4
    reorder = (source == wanted).astype(BF16)
    for h in range(heads):
        queries = tokens(first, own_ref, other_ref, 2 * heads + h)
        carried = dot(queries, prior_ref[h], 1, 0) * scale[:, h : h + 1]
        combined = local_ref[h] + carried
        square = jnp.mean(combined * combined, axis=-1, keepdims=True)
        normed = (combined * lax.rsqrt(square + 1e-05)).astype(BF16)
        normed = dot(normed, reorder, 1, 0).astype(BF16)
        keep_ref[h] = jnp.where(first, normed[:count], normed[count:])
        send_ref[h] = jnp.where(first, normed[count:], normed[:count])


def project_kernel(core_ref, kept_ref, got_ref, weight_ref, out_ref, rows_ref, sems):
    first = core_ref[0] == 0
    heads = rows_ref.shape[0]
    half = heads // 2
    lines = weight_ref.shape[0]

    def copy(h):
        source = weight_ref.at[h % lines, :, h // lines]
        return pltpu.make_async_copy(source, rows_ref.at[h], sems.at[h])

    def normed(h):
        low, high = both(first, kept_ref, got_ref, h % half)
        return low if h < half else high

    for h in range(heads):
        copy(h).start()
    acc = jnp.zeros(out_ref.shape, F32)
    for h in range(0, heads, RUN):
        run = range(h, h + RUN)
        for i in run:
            copy(i).wait()
        rows = rows_ref[h : h + RUN].reshape(RUN * HD, out_ref.shape[1])
        acc = acc + dot(jnp.concatenate([normed(i) for i in run], axis=1), rows, 1, 0)
    out_ref[...] = acc.astype(BF16)


def swap(x, within):
    return lax.all_to_all(
        x, ("seq", "head"), split_axis=0, concat_axis=0, axis_index_groups=within, tiled=True
    )


def shape(*dims, kind=F32):
    return jax.ShapeDtypeStruct(dims, kind)


def call(kernel, out, *args, **options):
    vmem = pl.BlockSpec(memory_space=pltpu.VMEM)
    smem = pl.BlockSpec(memory_space=pltpu.SMEM)
    return pl.pallas_call(
        kernel,
        out_shape=out,
        in_specs=[smem] + [vmem] * (len(args) - 1),
        out_specs=jax.tree.map(lambda _: vmem, out),
        compiler_params=VMEM,
        **options,
    )(*args)


def mix(queries, keys, values, log_decay, out_weight):
    count, width = queries.shape
    heads = log_decay.shape[1]
    half = heads // 2
    groups = lax.axis_size("seq")
    members = lax.axis_size("head")
    decay_t = log_decay.T
    devices = groups * members
    size = 2 * NEAR
    rows = HD * half // NEAR
    near = [list(range(i + c, i + size, 2)) for i in range(0, devices, size) for c in range(2)]
    far = [list(range(i, devices, size)) for i in range(size)]
    lanes = groups // ROW
    chips = members // 2

    def device(x, y, z, c):
        return (x * ROW + y) * members + 2 * z + c

    plane = [
        [device(x, y, z, c) for x in range(lanes) for z in range(chips)]
        for y in range(ROW)
        for c in range(2)
    ]
    ring = [
        [device(x, y, z, c) for y in range(ROW) for c in range(2)]
        for x in range(lanes)
        for z in range(chips)
    ]
    partner = [(i, i ^ 1) for i in range(members)]
    core = (lax.axis_index("head") & 1).reshape(1)
    place = (lax.axis_index("seq") // (size // members)).reshape(1)

    weight_rows = out_weight.shape[0]
    spread = pl.pallas_call(
        spread_kernel, out_shape=shape(groups, weight_rows, width, kind=BF16), compiler_params=VMEM
    )(out_weight)
    spread = swap(spread, plane)
    spread = pl.pallas_call(
        merge_kernel, out_shape=shape(groups * weight_rows, width, kind=BF16), compiler_params=VMEM
    )(spread)
    weight = lax.all_gather(
        spread, ("seq", "head"), axis=0, axis_index_groups=ring, tiled=True
    )

    pair = shape(3 * half + 1, count, HD, kind=BF16)
    own, other = call(pack_kernel, (pair, pair), core, decay_t, queries, keys, values)
    other = lax.ppermute(other, "head", partner)
    states = call(states_kernel, shape(NEAR, rows + PAD, HD, kind=BF16), core, own, other)
    local_part = call(local_kernel, shape(half, 2 * count, HD), core, own, other)
    group = swap(states, near)
    totals = pl.pallas_call(
        group_kernel,
        out_shape=shape(len(far[0]), rows + PAD, HD, kind=BF16),
        compiler_params=VMEM,
    )(group)
    totals = swap(totals, far)
    prior = call(prior_kernel, shape(NEAR, rows, HD, kind=BF16), place, totals, group)
    prior = swap(prior, near).reshape(half, HD, HD)
    normed = shape(half, count, HD, kind=BF16)
    kept, sent = call(norm_kernel, (normed, normed), core, own, other, local_part, prior)
    got = lax.ppermute(sent, "head", partner)
    run = chips * weight_rows
    weight = weight.reshape(ROW // 2, 4, lanes, run, width)
    weight = pltpu.with_memory_space_constraint(weight, pltpu.HBM)
    vmem = pl.BlockSpec(memory_space=pltpu.VMEM)
    return pl.pallas_call(
        project_kernel,
        out_shape=shape(count, width, kind=BF16),
        in_specs=[
            pl.BlockSpec(memory_space=pltpu.SMEM),
            vmem,
            vmem,
            pl.BlockSpec(memory_space=pltpu.HBM),
        ],
        out_specs=vmem,
        scratch_shapes=[
            pltpu.VMEM((heads, 4, run, width), BF16),
            pltpu.SemaphoreType.DMA((heads,)),
        ],
        compiler_params=LARGE,
    )(core, kept, got, weight)


def solution(mesh):
    placed = P(("seq", "head"), None)
    return jax.shard_map(mix, mesh=mesh, in_specs=(placed,) * 5, out_specs=placed, check_vma=False)
```

```python
import jax
import jax.numpy as jnp
from jax import lax
from jax.experimental import pallas as pl
from jax.experimental.pallas import tpu as pltpu
from jax.sharding import PartitionSpec as P

HD = 128
PAD = 8
NEAR = 16
RUN = 2
ROW = 8
BF16 = jnp.bfloat16
F32 = jnp.float32
VMEM = pltpu.CompilerParams(vmem_limit_bytes=12 * 1024 * 1024)
LARGE = pltpu.CompilerParams(vmem_limit_bytes=20 * 1024 * 1024)


def ones_below(rows):
    return (
        lax.broadcasted_iota(jnp.int32, (rows, rows), 0)
        >= lax.broadcasted_iota(jnp.int32, (rows, rows), 1)
    ).astype(BF16)


def dot(a, b, ca, cb):
    return lax.dot_general(a, b, (((ca,), (cb,)), ((), ())), preferred_element_type=F32)


def within_rows(decay_t):
    return dot(decay_t, ones_below(decay_t.shape[1]), 1, 1)


def within_cols(decay_t):
    return dot(ones_below(decay_t.shape[1]), decay_t, 1, 1)


def parts_of(total):
    row = lax.broadcasted_iota(jnp.int32, (PAD, HD), 0)
    whole = jnp.broadcast_to(total, (PAD, HD))
    high = whole.astype(BF16).astype(F32)
    middle = (whole - high).astype(BF16).astype(F32)
    low = whole - high - middle
    parts = jnp.where(row == 0, high, jnp.where(row == 1, middle, jnp.where(row == 2, low, 0.0)))
    return parts.astype(BF16)


def total_of(ref, i):
    parts = ref[i, ref.shape[1] - PAD :, :].astype(F32)
    return parts[0:1, :] + parts[1:2, :] + parts[2:3, :]


def spread_kernel(weight_ref, out_ref):
    for i in range(out_ref.shape[0]):
        out_ref[i] = weight_ref[...]


def merge_kernel(in_ref, out_ref):
    for i in range(0, in_ref.shape[0], 2):
        pair = jnp.concatenate([in_ref[i], in_ref[i + 1]], axis=0)
        out_ref[4 * i : 4 * i + 8, :] = pair


def pack_kernel(core_ref, decay_ref, queries_ref, keys_ref, values_ref, own_ref, other_ref):
    first = core_ref[0] == 0
    half = (own_ref.shape[0] - 1) // 3
    for n, ref in enumerate((keys_ref, values_ref, queries_ref)):
        for h in range(half):
            low = ref[:, h * HD : (h + 1) * HD]
            high = ref[:, (half + h) * HD : (half + h + 1) * HD]
            own_ref[n * half + h] = jnp.where(first, low, high)
            other_ref[n * half + h] = jnp.where(first, high, low)
    low = decay_ref[:half, :].astype(F32)
    high = decay_ref[half:, :].astype(F32)
    rest = jnp.zeros((HD - half, HD), F32)
    kept = jnp.concatenate([jnp.where(first, low, high), rest], axis=0)
    sent = jnp.concatenate([jnp.where(first, high, low), rest], axis=0)
    own_ref[3 * half] = kept.astype(BF16)
    other_ref[3 * half] = sent.astype(BF16)


def both(first, own_ref, other_ref, i):
    own, other = own_ref[i], other_ref[i]
    return jnp.where(first, own, other), jnp.where(first, other, own)


def tokens(first, own_ref, other_ref, i):
    return jnp.concatenate(both(first, own_ref, other_ref, i), axis=0)


def decays(first, own_ref, other_ref):
    half = (own_ref.shape[0] - 1) // 3
    early, late = both(first, own_ref, other_ref, 3 * half)
    return jnp.concatenate([early[:half, :], late[:half, :]], axis=1)


def states_kernel(core_ref, own_ref, other_ref, out_ref):
    first = core_ref[0] == 0
    heads = (own_ref.shape[0] - 1) // 3
    pieces = out_ref.shape[0] // heads
    rows = HD // pieces
    decay_t = decays(first, own_ref, other_ref)
    count = decay_t.shape[1]
    within = within_rows(decay_t)
    total = within[:, count - 1 : count]
    coef = jnp.exp(total - within)
    for h in range(heads):
        keys_t = tokens(first, own_ref, other_ref, h).astype(F32).T * coef[h : h + 1, :]
        values = tokens(first, own_ref, other_ref, heads + h)
        state = dot(keys_t.astype(BF16), values, 1, 0).astype(BF16)
        parts = parts_of(total[h : h + 1, :])
        for j in range(pieces):
            out_ref[h * pieces + j, :rows, :] = state[rows * j : rows * (j + 1), :]
            out_ref[h * pieces + j, rows:, :] = parts


def group_kernel(group_ref, out_ref):
    rows = group_ref.shape[1] - PAD
    state = jnp.zeros((rows, HD), F32)
    total = jnp.zeros((1, HD), F32)
    for i in range(group_ref.shape[0]):
        step = total_of(group_ref, i)
        state = jnp.exp(step) * state + group_ref[i, :rows, :].astype(F32)
        total = total + step
    state = state.astype(BF16)
    parts = parts_of(total)
    for j in range(out_ref.shape[0]):
        out_ref[j, :rows, :] = state
        out_ref[j, rows:, :] = parts


def prior_kernel(place_ref, planes_ref, lines_ref, group_ref, out_ref):
    rows = out_ref.shape[1]
    state = jnp.zeros((rows, HD), F32)
    for n, ref in enumerate((planes_ref, lines_ref)):
        for i in range(ref.shape[0]):
            later = jnp.exp(total_of(ref, i)) * state + ref[i, :rows, :].astype(F32)
            state = jnp.where(i < place_ref[n], later, state)
    for i in range(group_ref.shape[0]):
        out_ref[i] = state.astype(BF16)
        state = jnp.exp(total_of(group_ref, i)) * state + group_ref[i, :rows, :].astype(F32)


def local_kernel(core_ref, own_ref, other_ref, out_ref):
    first = core_ref[0] == 0
    heads, count, _ = out_ref.shape
    decay_t = decays(first, own_ref, other_ref)
    rows = within_rows(decay_t)
    cols = within_cols(decay_t)
    causal = lax.broadcasted_iota(jnp.int32, (count, count), 0) >= lax.broadcasted_iota(
        jnp.int32, (count, count), 1
    )
    for h in range(heads):
        keys = tokens(first, own_ref, other_ref, h)
        values = tokens(first, own_ref, other_ref, heads + h)
        queries = tokens(first, own_ref, other_ref, 2 * heads + h)
        scores = dot(queries, keys, 1, 1)
        gaps = cols[:, h : h + 1] - rows[h : h + 1, :]
        decay = jnp.exp(jnp.where(causal, gaps, -jnp.inf))
        weights = (scores * decay).astype(BF16)
        out_ref[h] = dot(weights, values, 1, 0)


def norm_kernel(core_ref, own_ref, other_ref, local_ref, prior_ref, keep_ref, send_ref):
    first = core_ref[0] == 0
    heads = local_ref.shape[0]
    count = keep_ref.shape[1]
    scale = jnp.exp(within_cols(decays(first, own_ref, other_ref)))
    place = lax.broadcasted_iota(jnp.int32, (HD, HD), 1)
    source = lax.broadcasted_iota(jnp.int32, (HD, HD), 0)
    wanted = (place // 64) * 64 + (place % 32 // 4) * 8 + (place // 32 % 2) * 4 + place % 4
    reorder = (source == wanted).astype(BF16)
    for h in range(heads):
        queries = tokens(first, own_ref, other_ref, 2 * heads + h)
        carried = dot(queries, prior_ref[h], 1, 0) * scale[:, h : h + 1]
        combined = local_ref[h] + carried
        square = jnp.mean(combined * combined, axis=-1, keepdims=True)
        normed = (combined * lax.rsqrt(square + 1e-05)).astype(BF16)
        normed = dot(normed, reorder, 1, 0).astype(BF16)
        keep_ref[h] = jnp.where(first, normed[:count], normed[count:])
        send_ref[h] = jnp.where(first, normed[count:], normed[:count])


def project_kernel(core_ref, kept_ref, got_ref, weight_ref, out_ref, rows_ref, sems):
    first = core_ref[0] == 0
    heads = rows_ref.shape[0]
    half = heads // 2
    lines = weight_ref.shape[0]

    def copy(h):
        source = weight_ref.at[h % lines, :, h // lines]
        return pltpu.make_async_copy(source, rows_ref.at[h], sems.at[h])

    def normed(h):
        low, high = both(first, kept_ref, got_ref, h % half)
        return low if h < half else high

    for h in range(heads):
        copy(h).start()
    acc = jnp.zeros(out_ref.shape, F32)
    for h in range(0, heads, RUN):
        run = range(h, h + RUN)
        for i in run:
            copy(i).wait()
        rows = rows_ref[h : h + RUN].reshape(RUN * HD, out_ref.shape[1])
        acc = acc + dot(jnp.concatenate([normed(i) for i in run], axis=1), rows, 1, 0)
    out_ref[...] = acc.astype(BF16)


def swap(x, within):
    return lax.all_to_all(
        x, ("seq", "head"), split_axis=0, concat_axis=0, axis_index_groups=within, tiled=True
    )


def shape(*dims, kind=F32):
    return jax.ShapeDtypeStruct(dims, kind)


def summed(group, copies):
    return pl.pallas_call(
        group_kernel,
        out_shape=shape(copies, *group.shape[1:], kind=BF16),
        compiler_params=VMEM,
    )(group)


def call(kernel, out, *args, **options):
    vmem = pl.BlockSpec(memory_space=pltpu.VMEM)
    smem = pl.BlockSpec(memory_space=pltpu.SMEM)
    return pl.pallas_call(
        kernel,
        out_shape=out,
        in_specs=[smem] + [vmem] * (len(args) - 1),
        out_specs=jax.tree.map(lambda _: vmem, out),
        compiler_params=VMEM,
        **options,
    )(*args)


def mix(queries, keys, values, log_decay, out_weight):
    count, width = queries.shape
    heads = log_decay.shape[1]
    half = heads // 2
    groups = lax.axis_size("seq")
    members = lax.axis_size("head")
    decay_t = log_decay.T
    devices = groups * members
    size = 2 * NEAR
    rows = HD * half // NEAR
    near = [list(range(i + c, i + size, 2)) for i in range(0, devices, size) for c in range(2)]
    lanes = groups // ROW
    chips = members // 2

    def device(x, y, z, c):
        return (x * ROW + y) * members + 2 * z + c

    plane = [
        [device(x, y, z, c) for x in range(lanes) for z in range(chips)]
        for y in range(ROW)
        for c in range(2)
    ]
    ring = [
        [device(x, y, z, c) for y in range(ROW) for c in range(2)]
        for x in range(lanes)
        for z in range(chips)
    ]
    pairs = size // members
    far = [
        [device(x, pairs * i + y, z, c) for i in range(ROW // pairs)]
        for x in range(lanes)
        for y in range(pairs)
        for z in range(chips)
        for c in range(2)
    ]
    across = [
        [device(x, y, z, c) for x in range(lanes)]
        for y in range(ROW)
        for z in range(chips)
        for c in range(2)
    ]
    seq = lax.axis_index("seq")
    place = jnp.stack([lax.div(seq, ROW), lax.div(lax.rem(seq, ROW), pairs)])
    partner = [(i, i ^ 1) for i in range(members)]
    core = (lax.axis_index("head") & 1).reshape(1)

    weight_rows = out_weight.shape[0]
    spread = pl.pallas_call(
        spread_kernel, out_shape=shape(groups, weight_rows, width, kind=BF16), compiler_params=VMEM
    )(out_weight)
    spread = swap(spread, plane)
    spread = pl.pallas_call(
        merge_kernel, out_shape=shape(groups * weight_rows, width, kind=BF16), compiler_params=VMEM
    )(spread)
    weight = lax.all_gather(
        spread, ("seq", "head"), axis=0, axis_index_groups=ring, tiled=True
    )

    pair = shape(3 * half + 1, count, HD, kind=BF16)
    own, other = call(pack_kernel, (pair, pair), core, decay_t, queries, keys, values)
    other = lax.ppermute(other, "head", partner)
    states = call(states_kernel, shape(NEAR, rows + PAD, HD, kind=BF16), core, own, other)
    local_part = call(local_kernel, shape(half, 2 * count, HD), core, own, other)
    group = swap(states, near)
    lines = swap(summed(group, len(far[0])), far)
    planes = swap(summed(lines, lanes), across)
    prior = call(prior_kernel, shape(NEAR, rows, HD, kind=BF16), place, planes, lines, group)
    prior = swap(prior, near).reshape(half, HD, HD)
    normed = shape(half, count, HD, kind=BF16)
    kept, sent = call(norm_kernel, (normed, normed), core, own, other, local_part, prior)
    got = lax.ppermute(sent, "head", partner)
    run = chips * weight_rows
    weight = weight.reshape(ROW // 2, 4, lanes, run, width)
    weight = pltpu.with_memory_space_constraint(weight, pltpu.HBM)
    vmem = pl.BlockSpec(memory_space=pltpu.VMEM)
    return pl.pallas_call(
        project_kernel,
        out_shape=shape(count, width, kind=BF16),
        in_specs=[
            pl.BlockSpec(memory_space=pltpu.SMEM),
            vmem,
            vmem,
            pl.BlockSpec(memory_space=pltpu.HBM),
        ],
        out_specs=vmem,
        scratch_shapes=[
            pltpu.VMEM((heads, 4, run, width), BF16),
            pltpu.SemaphoreType.DMA((heads,)),
        ],
        compiler_params=LARGE,
    )(core, kept, got, weight)


def solution(mesh):
    placed = P(("seq", "head"), None)
    return jax.shard_map(mix, mesh=mesh, in_specs=(placed,) * 5, out_specs=placed, check_vma=False)
```

```python
import jax
import jax.numpy as jnp
from jax import lax
from jax.experimental import pallas as pl
from jax.experimental.pallas import tpu as pltpu
from jax.sharding import PartitionSpec as P

HD = 128
PAD = 8
NEAR = 16
RUN = 2
ROW = 8
BF16 = jnp.bfloat16
F32 = jnp.float32
VMEM = pltpu.CompilerParams(vmem_limit_bytes=12 * 1024 * 1024)
LARGE = pltpu.CompilerParams(vmem_limit_bytes=20 * 1024 * 1024)


def ones_below(rows):
    return (
        lax.broadcasted_iota(jnp.int32, (rows, rows), 0)
        >= lax.broadcasted_iota(jnp.int32, (rows, rows), 1)
    ).astype(BF16)


def dot(a, b, ca, cb):
    return lax.dot_general(a, b, (((ca,), (cb,)), ((), ())), preferred_element_type=F32)


def within_rows(decay_t):
    return dot(decay_t, ones_below(decay_t.shape[1]), 1, 1)


def within_cols(decay_t):
    return dot(ones_below(decay_t.shape[1]), decay_t, 1, 1)


def parts_of(total):
    row = lax.broadcasted_iota(jnp.int32, (PAD, HD), 0)
    whole = jnp.broadcast_to(total, (PAD, HD))
    high = whole.astype(BF16).astype(F32)
    middle = (whole - high).astype(BF16).astype(F32)
    low = whole - high - middle
    parts = jnp.where(row == 0, high, jnp.where(row == 1, middle, jnp.where(row == 2, low, 0.0)))
    return parts.astype(BF16)


def total_of(ref, i):
    parts = ref[i, ref.shape[1] - PAD :, :].astype(F32)
    return parts[0:1, :] + parts[1:2, :] + parts[2:3, :]


def spread_kernel(weight_ref, out_ref):
    for i in range(out_ref.shape[0]):
        out_ref[i] = weight_ref[...]


def merge_kernel(in_ref, out_ref):
    for i in range(0, in_ref.shape[0], 2):
        pair = jnp.concatenate([in_ref[i], in_ref[i + 1]], axis=0)
        out_ref[4 * i : 4 * i + 8, :] = pair


def pack_kernel(core_ref, decay_ref, queries_ref, keys_ref, values_ref, own_ref, other_ref):
    first = core_ref[0] == 0
    half = (own_ref.shape[0] - 1) // 3
    for n, ref in enumerate((keys_ref, values_ref, queries_ref)):
        for h in range(half):
            low = ref[:, h * HD : (h + 1) * HD]
            high = ref[:, (half + h) * HD : (half + h + 1) * HD]
            own_ref[n * half + h] = jnp.where(first, low, high)
            other_ref[n * half + h] = jnp.where(first, high, low)
    low = decay_ref[:half, :].astype(F32)
    high = decay_ref[half:, :].astype(F32)
    rest = jnp.zeros((HD - half, HD), F32)
    kept = jnp.concatenate([jnp.where(first, low, high), rest], axis=0)
    sent = jnp.concatenate([jnp.where(first, high, low), rest], axis=0)
    own_ref[3 * half] = kept.astype(BF16)
    other_ref[3 * half] = sent.astype(BF16)


def both(first, own_ref, other_ref, i):
    own, other = own_ref[i], other_ref[i]
    return jnp.where(first, own, other), jnp.where(first, other, own)


def tokens(first, own_ref, other_ref, i):
    return jnp.concatenate(both(first, own_ref, other_ref, i), axis=0)


def decays(first, own_ref, other_ref):
    half = (own_ref.shape[0] - 1) // 3
    early, late = both(first, own_ref, other_ref, 3 * half)
    return jnp.concatenate([early[:half, :], late[:half, :]], axis=1)


def states_kernel(core_ref, own_ref, other_ref, out_ref):
    first = core_ref[0] == 0
    heads = (own_ref.shape[0] - 1) // 3
    pieces = out_ref.shape[0] // heads
    rows = HD // pieces
    decay_t = decays(first, own_ref, other_ref)
    count = decay_t.shape[1]
    within = within_rows(decay_t)
    total = within[:, count - 1 : count]
    coef = jnp.exp(total - within)
    for h in range(heads):
        keys_t = tokens(first, own_ref, other_ref, h).astype(F32).T * coef[h : h + 1, :]
        values = tokens(first, own_ref, other_ref, heads + h)
        state = dot(keys_t.astype(BF16), values, 1, 0).astype(BF16)
        parts = parts_of(total[h : h + 1, :])
        for j in range(pieces):
            out_ref[h * pieces + j, :rows, :] = state[rows * j : rows * (j + 1), :]
            out_ref[h * pieces + j, rows:, :] = parts


def total_state(ref, rows):
    state = jnp.zeros((rows, HD), F32)
    total = jnp.zeros((1, HD), F32)
    for i in range(ref.shape[0]):
        step = total_of(ref, i)
        state = jnp.exp(step) * state + ref[i, :rows, :].astype(F32)
        total = total + step
    return state.astype(BF16), parts_of(total)


def group_kernel(group_ref, out_ref):
    rows = out_ref.shape[0] - PAD
    out_ref[:rows, :], out_ref[rows:, :] = total_state(group_ref, rows)


def plane_kernel(place_ref, *refs):
    *group_refs, lines_ref, out_ref = refs
    count = len(group_refs)
    rows = lines_ref.shape[1] - PAD
    for i in range(count):
        away = lax.rem(place_ref[1] - i + count, count)
        group = group_refs[0][...]
        for k in range(1, count):
            group = jnp.where(away == k, group_refs[k][...], group)
        lines_ref[i] = group
    state, parts = total_state(lines_ref, rows)
    for j in range(out_ref.shape[0]):
        out_ref[j, :rows, :] = state
        out_ref[j, rows:, :] = parts


def prior_kernel(place_ref, planes_ref, lines_ref, group_ref, out_ref):
    rows = out_ref.shape[1]
    state = jnp.zeros((rows, HD), F32)
    for n, ref in enumerate((planes_ref, lines_ref)):
        for i in range(ref.shape[0]):
            later = jnp.exp(total_of(ref, i)) * state + ref[i, :rows, :].astype(F32)
            state = jnp.where(i < place_ref[n], later, state)
    for i in range(group_ref.shape[0]):
        out_ref[i] = state.astype(BF16)
        state = jnp.exp(total_of(group_ref, i)) * state + group_ref[i, :rows, :].astype(F32)


def local_kernel(core_ref, own_ref, other_ref, out_ref):
    first = core_ref[0] == 0
    heads, count, _ = out_ref.shape
    decay_t = decays(first, own_ref, other_ref)
    rows = within_rows(decay_t)
    cols = within_cols(decay_t)
    causal = lax.broadcasted_iota(jnp.int32, (count, count), 0) >= lax.broadcasted_iota(
        jnp.int32, (count, count), 1
    )
    for h in range(heads):
        keys = tokens(first, own_ref, other_ref, h)
        values = tokens(first, own_ref, other_ref, heads + h)
        queries = tokens(first, own_ref, other_ref, 2 * heads + h)
        scores = dot(queries, keys, 1, 1)
        gaps = cols[:, h : h + 1] - rows[h : h + 1, :]
        decay = jnp.exp(jnp.where(causal, gaps, -jnp.inf))
        weights = (scores * decay).astype(BF16)
        out_ref[h] = dot(weights, values, 1, 0)


def norm_kernel(core_ref, own_ref, other_ref, local_ref, prior_ref, keep_ref, send_ref):
    first = core_ref[0] == 0
    heads = local_ref.shape[0]
    count = keep_ref.shape[1]
    scale = jnp.exp(within_cols(decays(first, own_ref, other_ref)))
    place = lax.broadcasted_iota(jnp.int32, (HD, HD), 1)
    source = lax.broadcasted_iota(jnp.int32, (HD, HD), 0)
    wanted = (place // 64) * 64 + (place % 32 // 4) * 8 + (place // 32 % 2) * 4 + place % 4
    reorder = (source == wanted).astype(BF16)
    for h in range(heads):
        queries = tokens(first, own_ref, other_ref, 2 * heads + h)
        carried = dot(queries, prior_ref[h], 1, 0) * scale[:, h : h + 1]
        combined = local_ref[h] + carried
        square = jnp.mean(combined * combined, axis=-1, keepdims=True)
        normed = (combined * lax.rsqrt(square + 1e-05)).astype(BF16)
        normed = dot(normed, reorder, 1, 0).astype(BF16)
        keep_ref[h] = jnp.where(first, normed[:count], normed[count:])
        send_ref[h] = jnp.where(first, normed[count:], normed[:count])


def project_kernel(core_ref, kept_ref, got_ref, weight_ref, out_ref, rows_ref, sems):
    first = core_ref[0] == 0
    heads = rows_ref.shape[0]
    half = heads // 2
    lines = weight_ref.shape[0]

    def copy(h):
        source = weight_ref.at[h % lines, :, h // lines]
        return pltpu.make_async_copy(source, rows_ref.at[h], sems.at[h])

    def normed(h):
        low, high = both(first, kept_ref, got_ref, h % half)
        return low if h < half else high

    for h in range(heads):
        copy(h).start()
    acc = jnp.zeros(out_ref.shape, F32)
    for h in range(0, heads, RUN):
        run = range(h, h + RUN)
        for i in run:
            copy(i).wait()
        rows = rows_ref[h : h + RUN].reshape(RUN * HD, out_ref.shape[1])
        acc = acc + dot(jnp.concatenate([normed(i) for i in run], axis=1), rows, 1, 0)
    out_ref[...] = acc.astype(BF16)


def swap(x, within):
    return lax.all_to_all(
        x, ("seq", "head"), split_axis=0, concat_axis=0, axis_index_groups=within, tiled=True
    )


def shape(*dims, kind=F32):
    return jax.ShapeDtypeStruct(dims, kind)


def call(kernel, out, *args, **options):
    vmem = pl.BlockSpec(memory_space=pltpu.VMEM)
    smem = pl.BlockSpec(memory_space=pltpu.SMEM)
    return pl.pallas_call(
        kernel,
        out_shape=out,
        in_specs=[smem] + [vmem] * (len(args) - 1),
        out_specs=jax.tree.map(lambda _: vmem, out),
        compiler_params=VMEM,
        **options,
    )(*args)


def mix(queries, keys, values, log_decay, out_weight):
    count, width = queries.shape
    heads = log_decay.shape[1]
    half = heads // 2
    groups = lax.axis_size("seq")
    members = lax.axis_size("head")
    decay_t = log_decay.T
    devices = groups * members
    size = 2 * NEAR
    rows = HD * half // NEAR
    near = [list(range(i + c, i + size, 2)) for i in range(0, devices, size) for c in range(2)]
    lanes = groups // ROW
    chips = members // 2

    def device(x, y, z, c):
        return (x * ROW + y) * members + 2 * z + c

    plane = [
        [device(x, y, z, c) for x in range(lanes) for z in range(chips)]
        for y in range(ROW)
        for c in range(2)
    ]
    ring = [
        [device(x, y, z, c) for y in range(ROW) for c in range(2)]
        for x in range(lanes)
        for z in range(chips)
    ]
    pairs = size // members
    lines = ROW // pairs
    shifts = [
        [(x * ROW + y, x * ROW + (y + pairs * k) % ROW) for x in range(lanes) for y in range(ROW)]
        for k in range(1, lines)
    ]
    across = [
        [device(x, y, z, c) for x in range(lanes)]
        for y in range(ROW)
        for z in range(chips)
        for c in range(2)
    ]
    seq = lax.axis_index("seq")
    place = jnp.stack([lax.div(seq, ROW), lax.div(lax.rem(seq, ROW), pairs)])
    partner = [(i, i ^ 1) for i in range(members)]
    core = (lax.axis_index("head") & 1).reshape(1)

    weight_rows = out_weight.shape[0]
    spread = pl.pallas_call(
        spread_kernel, out_shape=shape(groups, weight_rows, width, kind=BF16), compiler_params=VMEM
    )(out_weight)
    spread = swap(spread, plane)
    spread = pl.pallas_call(
        merge_kernel, out_shape=shape(groups * weight_rows, width, kind=BF16), compiler_params=VMEM
    )(spread)
    weight = lax.all_gather(
        spread, ("seq", "head"), axis=0, axis_index_groups=ring, tiled=True
    )

    pair = shape(3 * half + 1, count, HD, kind=BF16)
    own, other = call(pack_kernel, (pair, pair), core, decay_t, queries, keys, values)
    other = lax.ppermute(other, "head", partner)
    states = call(states_kernel, shape(NEAR, rows + PAD, HD, kind=BF16), core, own, other)
    local_part = call(local_kernel, shape(half, 2 * count, HD), core, own, other)
    group = swap(states, near)
    own_sum = pl.pallas_call(
        group_kernel, out_shape=shape(rows + PAD, HD, kind=BF16), compiler_params=VMEM
    )(group)
    sums = [own_sum] + [lax.ppermute(own_sum, "seq", shift) for shift in shifts]
    outs = tuple(shape(n, rows + PAD, HD, kind=BF16) for n in (lines, lanes))
    in_order, planes = call(plane_kernel, outs, place, *sums)
    planes = swap(planes, across)
    prior = call(prior_kernel, shape(NEAR, rows, HD, kind=BF16), place, planes, in_order, group)
    prior = swap(prior, near).reshape(half, HD, HD)
    normed = shape(half, count, HD, kind=BF16)
    kept, sent = call(norm_kernel, (normed, normed), core, own, other, local_part, prior)
    got = lax.ppermute(sent, "head", partner)
    run = chips * weight_rows
    weight = weight.reshape(ROW // 2, 4, lanes, run, width)
    weight = pltpu.with_memory_space_constraint(weight, pltpu.HBM)
    vmem = pl.BlockSpec(memory_space=pltpu.VMEM)
    return pl.pallas_call(
        project_kernel,
        out_shape=shape(count, width, kind=BF16),
        in_specs=[
            pl.BlockSpec(memory_space=pltpu.SMEM),
            vmem,
            vmem,
            pl.BlockSpec(memory_space=pltpu.HBM),
        ],
        out_specs=vmem,
        scratch_shapes=[
            pltpu.VMEM((heads, 4, run, width), BF16),
            pltpu.SemaphoreType.DMA((heads,)),
        ],
        compiler_params=LARGE,
    )(core, kept, got, weight)


def solution(mesh):
    placed = P(("seq", "head"), None)
    return jax.shard_map(mix, mesh=mesh, in_specs=(placed,) * 5, out_specs=placed, check_vma=False)
```

```python
import jax
import jax.numpy as jnp
from jax import lax
from jax.experimental import pallas as pl
from jax.experimental.pallas import tpu as pltpu
from jax.sharding import PartitionSpec as P

HD = 128
PAD = 8
NEAR = 16
RUN = 2
ROW = 8
BF16 = jnp.bfloat16
F32 = jnp.float32
VMEM = pltpu.CompilerParams(vmem_limit_bytes=12 * 1024 * 1024)
LARGE = pltpu.CompilerParams(vmem_limit_bytes=20 * 1024 * 1024)


def ones_below(rows):
    return (
        lax.broadcasted_iota(jnp.int32, (rows, rows), 0)
        >= lax.broadcasted_iota(jnp.int32, (rows, rows), 1)
    ).astype(BF16)


def dot(a, b, ca, cb):
    return lax.dot_general(a, b, (((ca,), (cb,)), ((), ())), preferred_element_type=F32)


def within_rows(decay_t):
    return dot(decay_t, ones_below(decay_t.shape[1]), 1, 1)


def within_cols(decay_t):
    return dot(ones_below(decay_t.shape[1]), decay_t, 1, 1)


def parts_of(total):
    row = lax.broadcasted_iota(jnp.int32, (PAD, HD), 0)
    whole = jnp.broadcast_to(total, (PAD, HD))
    high = whole.astype(BF16).astype(F32)
    middle = (whole - high).astype(BF16).astype(F32)
    low = whole - high - middle
    parts = jnp.where(row == 0, high, jnp.where(row == 1, middle, jnp.where(row == 2, low, 0.0)))
    return parts.astype(BF16)


def total_of(ref, i):
    parts = ref[i, ref.shape[1] - PAD :, :].astype(F32)
    return parts[0:1, :] + parts[1:2, :] + parts[2:3, :]


def spread_kernel(weight_ref, out_ref, sems):
    def copy(i):
        return pltpu.make_async_copy(weight_ref, out_ref.at[i], sems.at[i])

    for i in range(out_ref.shape[0]):
        copy(i).start()
    for i in range(out_ref.shape[0]):
        copy(i).wait()


def merge_kernel(in_ref, out_ref, work_ref, sems):
    count = sems.shape[0]
    rows = out_ref.shape[0] // count

    def copy(n):
        part = pl.ds(n * rows, rows)
        return pltpu.make_async_copy(work_ref.at[part], out_ref.at[part], sems.at[n])

    for n in range(count):
        for row in range(n * rows, (n + 1) * rows, 8):
            pair = jnp.concatenate([in_ref[row // 4], in_ref[row // 4 + 1]], axis=0)
            work_ref[row : row + 8, :] = pair
        copy(n).start()
    for n in range(count):
        copy(n).wait()


def pack_kernel(core_ref, decay_ref, queries_ref, keys_ref, values_ref, own_ref, other_ref):
    first = core_ref[0] == 0
    half = (own_ref.shape[0] - 1) // 3
    place = lax.broadcasted_iota(jnp.int32, (HD, HD), 1)
    source = lax.broadcasted_iota(jnp.int32, (HD, HD), 0)
    wanted = (place // 64) * 64 + (place % 32 // 4) * 8 + (place // 32 % 2) * 4 + place % 4
    reorder = (source == wanted).astype(BF16)
    for n, ref in enumerate((keys_ref, values_ref, queries_ref)):
        for h in range(half):
            low = ref[:, h * HD : (h + 1) * HD]
            high = ref[:, (half + h) * HD : (half + h + 1) * HD]
            if ref is values_ref:
                low = dot(low, reorder, 1, 0).astype(BF16)
                high = dot(high, reorder, 1, 0).astype(BF16)
            own_ref[n * half + h] = jnp.where(first, low, high)
            other_ref[n * half + h] = jnp.where(first, high, low)
    low = decay_ref[:half, :].astype(F32)
    high = decay_ref[half:, :].astype(F32)
    rest = jnp.zeros((HD - half, HD), F32)
    kept = jnp.concatenate([jnp.where(first, low, high), rest], axis=0)
    sent = jnp.concatenate([jnp.where(first, high, low), rest], axis=0)
    own_ref[3 * half] = kept.astype(BF16)
    other_ref[3 * half] = sent.astype(BF16)


def both(first, own_ref, other_ref, i):
    own, other = own_ref[i], other_ref[i]
    return jnp.where(first, own, other), jnp.where(first, other, own)


def tokens(first, own_ref, other_ref, i):
    return jnp.concatenate(both(first, own_ref, other_ref, i), axis=0)


def decays(first, own_ref, other_ref):
    half = (own_ref.shape[0] - 1) // 3
    early, late = both(first, own_ref, other_ref, 3 * half)
    return jnp.concatenate([early[:half, :], late[:half, :]], axis=1)


def states_kernel(core_ref, own_ref, other_ref, out_ref):
    first = core_ref[0] == 0
    heads = (own_ref.shape[0] - 1) // 3
    pieces = out_ref.shape[0] // heads
    rows = HD // pieces
    decay_t = decays(first, own_ref, other_ref)
    count = decay_t.shape[1]
    within = within_rows(decay_t)
    total = within[:, count - 1 : count]
    coef = jnp.exp(total - within)
    for h in range(heads):
        keys_t = tokens(first, own_ref, other_ref, h).astype(F32).T * coef[h : h + 1, :]
        values = tokens(first, own_ref, other_ref, heads + h)
        state = dot(keys_t.astype(BF16), values, 1, 0).astype(BF16)
        parts = parts_of(total[h : h + 1, :])
        for j in range(pieces):
            out_ref[h * pieces + j, :rows, :] = state[rows * j : rows * (j + 1), :]
            out_ref[h * pieces + j, rows:, :] = parts


def group_kernel(group_ref, out_ref):
    rows = group_ref.shape[1] - PAD
    state = jnp.zeros((rows, HD), F32)
    total = jnp.zeros((1, HD), F32)
    for i in range(group_ref.shape[0]):
        step = total_of(group_ref, i)
        state = jnp.exp(step) * state + group_ref[i, :rows, :].astype(F32)
        total = total + step
    state = state.astype(BF16)
    parts = parts_of(total)
    for j in range(out_ref.shape[0]):
        out_ref[j, :rows, :] = state
        out_ref[j, rows:, :] = parts


def prior_kernel(place_ref, planes_ref, lines_ref, group_ref, out_ref):
    rows = out_ref.shape[1]
    state = jnp.zeros((rows, HD), F32)
    for n, ref in enumerate((planes_ref, lines_ref)):
        for i in range(ref.shape[0]):
            later = jnp.exp(total_of(ref, i)) * state + ref[i, :rows, :].astype(F32)
            state = jnp.where(i < place_ref[1 + n], later, state)
    for i in range(group_ref.shape[0]):
        out_ref[i] = state.astype(BF16)
        state = jnp.exp(total_of(group_ref, i)) * state + group_ref[i, :rows, :].astype(F32)


def local_kernel(core_ref, own_ref, other_ref, out_ref):
    first = core_ref[0] == 0
    heads, count, _ = out_ref.shape
    decay_t = decays(first, own_ref, other_ref)
    rows = within_rows(decay_t)
    cols = within_cols(decay_t)
    causal = lax.broadcasted_iota(jnp.int32, (count, count), 0) >= lax.broadcasted_iota(
        jnp.int32, (count, count), 1
    )
    for h in range(heads):
        keys = tokens(first, own_ref, other_ref, h)
        values = tokens(first, own_ref, other_ref, heads + h)
        queries = tokens(first, own_ref, other_ref, 2 * heads + h)
        scores = dot(queries, keys, 1, 1)
        gaps = cols[:, h : h + 1] - rows[h : h + 1, :]
        decay = jnp.exp(jnp.where(causal, gaps, -jnp.inf))
        weights = (scores * decay).astype(BF16)
        out_ref[h] = dot(weights, values, 1, 0)


def norm_kernel(core_ref, own_ref, other_ref, local_ref, prior_ref, keep_ref, send_ref):
    first = core_ref[0] == 0
    heads = local_ref.shape[0]
    count = keep_ref.shape[1]
    scale = jnp.exp(within_cols(decays(first, own_ref, other_ref)))
    for h in range(heads):
        queries = tokens(first, own_ref, other_ref, 2 * heads + h)
        carried = dot(queries, prior_ref[h], 1, 0) * scale[:, h : h + 1]
        combined = local_ref[h] + carried
        square = jnp.mean(combined * combined, axis=-1, keepdims=True)
        normed = (combined * lax.rsqrt(square + 1e-05)).astype(BF16)
        keep_ref[h] = jnp.where(first, normed[:count], normed[count:])
        send_ref[h] = jnp.where(first, normed[count:], normed[:count])


def project_kernel(core_ref, kept_ref, got_ref, weight_ref, out_ref, rows_ref, sems):
    first = core_ref[0] == 0
    heads = rows_ref.shape[0]
    half = heads // 2
    lines = weight_ref.shape[0]

    def copy(h):
        source = weight_ref.at[h % lines, :, h // lines]
        return pltpu.make_async_copy(source, rows_ref.at[h], sems.at[h])

    def normed(h):
        low, high = both(first, kept_ref, got_ref, h % half)
        return low if h < half else high

    for h in range(heads):
        copy(h).start()
    acc = jnp.zeros(out_ref.shape, F32)
    for h in range(0, heads, RUN):
        run = range(h, h + RUN)
        for i in run:
            copy(i).wait()
        rows = rows_ref[h : h + RUN].reshape(RUN * HD, out_ref.shape[1])
        acc = acc + dot(jnp.concatenate([normed(i) for i in run], axis=1), rows, 1, 0)
    out_ref[...] = acc.astype(BF16)


def swap(x, within):
    return lax.all_to_all(
        x, ("seq", "head"), split_axis=0, concat_axis=0, axis_index_groups=within, tiled=True
    )


def shape(*dims, kind=F32):
    return jax.ShapeDtypeStruct(dims, kind)


def summed(group, copies):
    return pl.pallas_call(
        group_kernel,
        out_shape=shape(copies, *group.shape[1:], kind=BF16),
        compiler_params=VMEM,
    )(group)


def call(kernel, out, *args, **options):
    vmem = pl.BlockSpec(memory_space=pltpu.VMEM)
    smem = pl.BlockSpec(memory_space=pltpu.SMEM)
    return pl.pallas_call(
        kernel,
        out_shape=out,
        in_specs=[smem] + [vmem] * (len(args) - 1),
        out_specs=jax.tree.map(lambda _: vmem, out),
        compiler_params=VMEM,
        **options,
    )(*args)


def mix(queries, keys, values, log_decay, out_weight):
    count, width = queries.shape
    heads = log_decay.shape[1]
    half = heads // 2
    groups = lax.axis_size("seq")
    members = lax.axis_size("head")
    decay_t = log_decay.T
    devices = groups * members
    size = 2 * NEAR
    rows = HD * half // NEAR
    near = [list(range(i + c, i + size, 2)) for i in range(0, devices, size) for c in range(2)]
    lanes = groups // ROW
    chips = members // 2

    def device(x, y, z, c):
        return (x * ROW + y) * members + 2 * z + c

    plane = [
        [device(x, y, z, c) for x in range(lanes) for z in range(chips)]
        for y in range(ROW)
        for c in range(2)
    ]
    ring = [
        [device(x, y, z, c) for y in range(ROW) for c in range(2)]
        for x in range(lanes)
        for z in range(chips)
    ]
    pairs = size // members
    far = [
        [device(x, pairs * i + y, z, c) for i in range(ROW // pairs)]
        for x in range(lanes)
        for y in range(pairs)
        for z in range(chips)
        for c in range(2)
    ]
    across = [
        [device(x, y, z, c) for x in range(lanes)]
        for y in range(ROW)
        for z in range(chips)
        for c in range(2)
    ]
    partner = [(i, i ^ 1) for i in range(members)]
    seq = lax.axis_index("seq")
    core = lax.rem(lax.axis_index("head"), 2)
    core = jnp.stack([core, lax.div(seq, ROW), lax.div(lax.rem(seq, ROW), pairs)])

    weight_rows = out_weight.shape[0]
    spread = pl.pallas_call(
        spread_kernel,
        out_shape=pltpu.HBM((groups, weight_rows, width), BF16),
        out_specs=pl.BlockSpec(memory_space=pltpu.HBM),
        scratch_shapes=[pltpu.SemaphoreType.DMA((groups,))],
        compiler_params=VMEM,
    )(out_weight)
    spread = swap(spread, plane)
    spread = pl.pallas_call(
        merge_kernel,
        out_shape=pltpu.HBM((groups * weight_rows, width), BF16),
        out_specs=pl.BlockSpec(memory_space=pltpu.HBM),
        scratch_shapes=[
            pltpu.VMEM((groups * weight_rows, width), BF16),
            pltpu.SemaphoreType.DMA((4,)),
        ],
        compiler_params=VMEM,
    )(spread)
    weight = lax.all_gather(
        spread, ("seq", "head"), axis=0, axis_index_groups=ring, tiled=True
    )

    pair = shape(3 * half + 1, count, HD, kind=BF16)
    own, other = call(pack_kernel, (pair, pair), core, decay_t, queries, keys, values)
    other = lax.ppermute(other, "head", partner)
    states = call(states_kernel, shape(NEAR, rows + PAD, HD, kind=BF16), core, own, other)
    local_part = call(local_kernel, shape(half, 2 * count, HD), core, own, other)
    group = swap(states, near)
    lines = swap(summed(group, len(far[0])), far)
    planes = swap(summed(lines, lanes), across)
    prior = call(prior_kernel, shape(NEAR, rows, HD, kind=BF16), core, planes, lines, group)
    prior = swap(prior, near).reshape(half, HD, HD)
    normed = shape(half, count, HD, kind=BF16)
    kept, sent = call(norm_kernel, (normed, normed), core, own, other, local_part, prior)
    got = lax.ppermute(sent, "head", partner)
    run = chips * weight_rows
    weight = weight.reshape(ROW // 2, 4, lanes, run, width)
    weight = pltpu.with_memory_space_constraint(weight, pltpu.HBM)
    vmem = pl.BlockSpec(memory_space=pltpu.VMEM)
    return pl.pallas_call(
        project_kernel,
        out_shape=shape(count, width, kind=BF16),
        in_specs=[
            pl.BlockSpec(memory_space=pltpu.SMEM),
            vmem,
            vmem,
            pl.BlockSpec(memory_space=pltpu.HBM),
        ],
        out_specs=vmem,
        scratch_shapes=[
            pltpu.VMEM((heads, 4, run, width), BF16),
            pltpu.SemaphoreType.DMA((heads,)),
        ],
        compiler_params=LARGE,
    )(core, kept, got, weight)


def solution(mesh):
    placed = P(("seq", "head"), None)
    return jax.shard_map(mix, mesh=mesh, in_specs=(placed,) * 5, out_specs=placed, check_vma=False)
```

```python
import jax
import jax.numpy as jnp
from jax import lax
from jax.experimental import pallas as pl
from jax.experimental.pallas import tpu as pltpu
from jax.sharding import PartitionSpec as P

HD = 128
PAD = 8
NEAR = 16
RUN = 2
ROW = 8
BF16 = jnp.bfloat16
F32 = jnp.float32
VMEM = pltpu.CompilerParams(vmem_limit_bytes=12 * 1024 * 1024)
LARGE = pltpu.CompilerParams(vmem_limit_bytes=20 * 1024 * 1024)


def ones_below(rows):
    return (
        lax.broadcasted_iota(jnp.int32, (rows, rows), 0)
        >= lax.broadcasted_iota(jnp.int32, (rows, rows), 1)
    ).astype(BF16)


def dot(a, b, ca, cb):
    return lax.dot_general(a, b, (((ca,), (cb,)), ((), ())), preferred_element_type=F32)


def within_rows(decay_t):
    return dot(decay_t, ones_below(decay_t.shape[1]), 1, 1)


def within_cols(decay_t):
    return dot(ones_below(decay_t.shape[1]), decay_t, 1, 1)


def parts_of(total):
    row = lax.broadcasted_iota(jnp.int32, (PAD, HD), 0)
    whole = jnp.broadcast_to(total, (PAD, HD))
    high = whole.astype(BF16).astype(F32)
    middle = (whole - high).astype(BF16).astype(F32)
    low = whole - high - middle
    parts = jnp.where(row == 0, high, jnp.where(row == 1, middle, jnp.where(row == 2, low, 0.0)))
    return parts.astype(BF16)


def total_of(ref, i):
    parts = ref[i, ref.shape[1] - PAD :, :].astype(F32)
    return parts[0:1, :] + parts[1:2, :] + parts[2:3, :]


def spread_kernel(weight_ref, out_ref):
    for i in range(out_ref.shape[0]):
        out_ref[i] = weight_ref[...]


def merge_kernel(in_ref, out_ref, work_ref, sems):
    count = sems.shape[0]
    rows = out_ref.shape[0] // count

    def copy(n):
        part = pl.ds(n * rows, rows)
        return pltpu.make_async_copy(work_ref.at[part], out_ref.at[part], sems.at[n])

    for n in range(count):
        for row in range(n * rows, (n + 1) * rows, 8):
            pair = jnp.concatenate([in_ref[row // 4], in_ref[row // 4 + 1]], axis=0)
            work_ref[row : row + 8, :] = pair
        copy(n).start()
    for n in range(count):
        copy(n).wait()


def pack_kernel(core_ref, plane_ref, line_ref, decay_ref, queries_ref, keys_ref, values_ref, own_ref, other_ref):
    first = core_ref[0] == 0
    half = (own_ref.shape[0] - 1) // 3
    place = lax.broadcasted_iota(jnp.int32, (HD, HD), 1)
    source = lax.broadcasted_iota(jnp.int32, (HD, HD), 0)
    wanted = (place // 64) * 64 + (place % 32 // 4) * 8 + (place // 32 % 2) * 4 + place % 4
    reorder = (source == wanted).astype(BF16)
    for n, ref in enumerate((keys_ref, values_ref, queries_ref)):
        for h in range(half):
            low = ref[:, h * HD : (h + 1) * HD]
            high = ref[:, (half + h) * HD : (half + h + 1) * HD]
            if ref is values_ref:
                low = dot(low, reorder, 1, 0).astype(BF16)
                high = dot(high, reorder, 1, 0).astype(BF16)
            own_ref[n * half + h] = jnp.where(first, low, high)
            other_ref[n * half + h] = jnp.where(first, high, low)
    low = decay_ref[:half, :].astype(F32)
    high = decay_ref[half:, :].astype(F32)
    rest = jnp.zeros((HD - half, HD), F32)
    kept = jnp.concatenate([jnp.where(first, low, high), rest], axis=0)
    sent = jnp.concatenate([jnp.where(first, high, low), rest], axis=0)
    own_ref[3 * half] = kept.astype(BF16)
    other_ref[3 * half] = sent.astype(BF16)


def both(first, own_ref, other_ref, i):
    own, other = own_ref[i], other_ref[i]
    return jnp.where(first, own, other), jnp.where(first, other, own)


def tokens(first, own_ref, other_ref, i):
    return jnp.concatenate(both(first, own_ref, other_ref, i), axis=0)


def decays(first, own_ref, other_ref):
    half = (own_ref.shape[0] - 1) // 3
    early, late = both(first, own_ref, other_ref, 3 * half)
    return jnp.concatenate([early[:half, :], late[:half, :]], axis=1)


def states_kernel(core_ref, own_ref, other_ref, out_ref):
    first = core_ref[0] == 0
    heads = (own_ref.shape[0] - 1) // 3
    pieces = out_ref.shape[0] // heads
    rows = HD // pieces
    decay_t = decays(first, own_ref, other_ref)
    count = decay_t.shape[1]
    within = within_rows(decay_t)
    total = within[:, count - 1 : count]
    coef = jnp.exp(total - within)
    for h in range(heads):
        keys_t = tokens(first, own_ref, other_ref, h).astype(F32).T * coef[h : h + 1, :]
        values = tokens(first, own_ref, other_ref, heads + h)
        state = dot(keys_t.astype(BF16), values, 1, 0).astype(BF16)
        parts = parts_of(total[h : h + 1, :])
        for j in range(pieces):
            out_ref[h * pieces + j, :rows, :] = state[rows * j : rows * (j + 1), :]
            out_ref[h * pieces + j, rows:, :] = parts


def group_kernel(group_ref, out_ref):
    rows = group_ref.shape[1] - PAD
    state = jnp.zeros((rows, HD), F32)
    total = jnp.zeros((1, HD), F32)
    for i in range(group_ref.shape[0]):
        step = total_of(group_ref, i)
        state = jnp.exp(step) * state + group_ref[i, :rows, :].astype(F32)
        total = total + step
    state = state.astype(BF16)
    parts = parts_of(total)
    for j in range(out_ref.shape[0]):
        out_ref[j, :rows, :] = state
        out_ref[j, rows:, :] = parts


def prior_kernel(plane_ref, line_ref, planes_ref, lines_ref, group_ref, out_ref):
    rows = out_ref.shape[1]
    state = jnp.zeros((rows, HD), F32)
    for place_ref, ref in ((plane_ref, planes_ref), (line_ref, lines_ref)):
        for i in range(ref.shape[0]):
            later = jnp.exp(total_of(ref, i)) * state + ref[i, :rows, :].astype(F32)
            state = jnp.where(i < place_ref[0], later, state)
    for i in range(group_ref.shape[0]):
        out_ref[i] = state.astype(BF16)
        state = jnp.exp(total_of(group_ref, i)) * state + group_ref[i, :rows, :].astype(F32)


def local_kernel(core_ref, own_ref, other_ref, out_ref):
    first = core_ref[0] == 0
    heads, count, _ = out_ref.shape
    decay_t = decays(first, own_ref, other_ref)
    rows = within_rows(decay_t)
    cols = within_cols(decay_t)
    causal = lax.broadcasted_iota(jnp.int32, (count, count), 0) >= lax.broadcasted_iota(
        jnp.int32, (count, count), 1
    )
    for h in range(heads):
        keys = tokens(first, own_ref, other_ref, h)
        values = tokens(first, own_ref, other_ref, heads + h)
        queries = tokens(first, own_ref, other_ref, 2 * heads + h)
        scores = dot(queries, keys, 1, 1)
        gaps = cols[:, h : h + 1] - rows[h : h + 1, :]
        decay = jnp.exp(jnp.where(causal, gaps, -jnp.inf))
        weights = (scores * decay).astype(BF16)
        out_ref[h] = dot(weights, values, 1, 0)


def norm_kernel(core_ref, own_ref, other_ref, local_ref, prior_ref, keep_ref, send_ref):
    first = core_ref[0] == 0
    heads = local_ref.shape[0]
    count = keep_ref.shape[1]
    scale = jnp.exp(within_cols(decays(first, own_ref, other_ref)))
    for h in range(heads):
        queries = tokens(first, own_ref, other_ref, 2 * heads + h)
        carried = dot(queries, prior_ref[h], 1, 0) * scale[:, h : h + 1]
        combined = local_ref[h] + carried
        square = jnp.mean(combined * combined, axis=-1, keepdims=True)
        normed = (combined * lax.rsqrt(square + 1e-05)).astype(BF16)
        keep_ref[h] = jnp.where(first, normed[:count], normed[count:])
        send_ref[h] = jnp.where(first, normed[count:], normed[:count])


def project_kernel(core_ref, kept_ref, got_ref, weight_ref, out_ref, rows_ref, sems):
    first = core_ref[0] == 0
    heads = rows_ref.shape[0]
    half = heads // 2
    lines = weight_ref.shape[0]

    def copy(h):
        source = weight_ref.at[h % lines, :, h // lines]
        return pltpu.make_async_copy(source, rows_ref.at[h], sems.at[h])

    def normed(h):
        low, high = both(first, kept_ref, got_ref, h % half)
        return low if h < half else high

    for h in range(heads):
        copy(h).start()
    acc = jnp.zeros(out_ref.shape, F32)
    for h in range(0, heads, RUN):
        run = range(h, h + RUN)
        for i in run:
            copy(i).wait()
        rows = rows_ref[h : h + RUN].reshape(RUN * HD, out_ref.shape[1])
        acc = acc + dot(jnp.concatenate([normed(i) for i in run], axis=1), rows, 1, 0)
    out_ref[...] = acc.astype(BF16)


def swap(x, within):
    return lax.all_to_all(
        x, ("seq", "head"), split_axis=0, concat_axis=0, axis_index_groups=within, tiled=True
    )


def shape(*dims, kind=F32):
    return jax.ShapeDtypeStruct(dims, kind)


def summed(group, copies):
    return pl.pallas_call(
        group_kernel,
        out_shape=shape(copies, *group.shape[1:], kind=BF16),
        compiler_params=VMEM,
    )(group)


def call(kernel, out, *args, **options):
    vmem = pl.BlockSpec(memory_space=pltpu.VMEM)
    smem = pl.BlockSpec(memory_space=pltpu.SMEM)
    return pl.pallas_call(
        kernel,
        out_shape=out,
        in_specs=[smem if a.dtype == jnp.int32 else vmem for a in args],
        out_specs=jax.tree.map(lambda _: vmem, out),
        compiler_params=VMEM,
        **options,
    )(*args)


def mix(queries, keys, values, log_decay, out_weight):
    count, width = queries.shape
    heads = log_decay.shape[1]
    half = heads // 2
    groups = lax.axis_size("seq")
    members = lax.axis_size("head")
    decay_t = log_decay.T
    devices = groups * members
    size = 2 * NEAR
    rows = HD * half // NEAR
    near = [list(range(i + c, i + size, 2)) for i in range(0, devices, size) for c in range(2)]
    lanes = groups // ROW
    chips = members // 2

    def device(x, y, z, c):
        return (x * ROW + y) * members + 2 * z + c

    plane = [
        [device(x, y, z, c) for x in range(lanes) for z in range(chips)]
        for y in range(ROW)
        for c in range(2)
    ]
    ring = [
        [device(x, y, z, c) for y in range(ROW) for c in range(2)]
        for x in range(lanes)
        for z in range(chips)
    ]
    pairs = size // members
    far = [
        [device(x, pairs * i + y, z, c) for i in range(ROW // pairs)]
        for x in range(lanes)
        for y in range(pairs)
        for z in range(chips)
        for c in range(2)
    ]
    across = [
        [device(x, y, z, c) for x in range(lanes)]
        for y in range(ROW)
        for z in range(chips)
        for c in range(2)
    ]
    partner = [(i, i ^ 1) for i in range(members)]
    seq = lax.axis_index("seq")
    core = lax.rem(lax.axis_index("head"), 2)
    core = core.reshape(1)
    plane_place = lax.div(seq, ROW).reshape(1)
    line_place = lax.div(lax.rem(seq, ROW), pairs).reshape(1)
    places = (plane_place, line_place)

    weight_rows = out_weight.shape[0]
    spread = pl.pallas_call(
        spread_kernel, out_shape=shape(groups, weight_rows, width, kind=BF16), compiler_params=VMEM
    )(out_weight)
    spread = swap(spread, plane)
    spread = pl.pallas_call(
        merge_kernel,
        out_shape=pltpu.HBM((groups * weight_rows, width), BF16),
        out_specs=pl.BlockSpec(memory_space=pltpu.HBM),
        scratch_shapes=[
            pltpu.VMEM((groups * weight_rows, width), BF16),
            pltpu.SemaphoreType.DMA((4,)),
        ],
        compiler_params=VMEM,
    )(spread)
    weight = lax.all_gather(
        spread, ("seq", "head"), axis=0, axis_index_groups=ring, tiled=True
    )

    pair = shape(3 * half + 1, count, HD, kind=BF16)
    own, other = call(pack_kernel, (pair, pair), core, *places, decay_t, queries, keys, values)
    other = lax.ppermute(other, "head", partner)
    states = call(states_kernel, shape(NEAR, rows + PAD, HD, kind=BF16), core, own, other)
    local_part = call(local_kernel, shape(half, 2 * count, HD), core, own, other)
    group = swap(states, near)
    lines = swap(summed(group, len(far[0])), far)
    planes = swap(summed(lines, lanes), across)
    prior = call(prior_kernel, shape(NEAR, rows, HD, kind=BF16), *places, planes, lines, group)
    prior = swap(prior, near).reshape(half, HD, HD)
    normed = shape(half, count, HD, kind=BF16)
    kept, sent = call(norm_kernel, (normed, normed), core, own, other, local_part, prior)
    got = lax.ppermute(sent, "head", partner)
    run = chips * weight_rows
    weight = weight.reshape(ROW // 2, 4, lanes, run, width)
    weight = pltpu.with_memory_space_constraint(weight, pltpu.HBM)
    vmem = pl.BlockSpec(memory_space=pltpu.VMEM)
    return pl.pallas_call(
        project_kernel,
        out_shape=shape(count, width, kind=BF16),
        in_specs=[
            pl.BlockSpec(memory_space=pltpu.SMEM),
            vmem,
            vmem,
            pl.BlockSpec(memory_space=pltpu.HBM),
        ],
        out_specs=vmem,
        scratch_shapes=[
            pltpu.VMEM((heads, 4, run, width), BF16),
            pltpu.SemaphoreType.DMA((heads,)),
        ],
        compiler_params=LARGE,
    )(core, kept, got, weight)


def solution(mesh):
    placed = P(("seq", "head"), None)
    return jax.shard_map(mix, mesh=mesh, in_specs=(placed,) * 5, out_specs=placed, check_vma=False)
```

```python
import jax
import jax.numpy as jnp
from jax import lax
from jax.experimental import pallas as pl
from jax.experimental.pallas import tpu as pltpu
from jax.sharding import PartitionSpec as P

HD = 128
PAD = 8
NEAR = 16
RUN = 2
ROW = 8
BF16 = jnp.bfloat16
F32 = jnp.float32
VMEM = pltpu.CompilerParams(vmem_limit_bytes=12 * 1024 * 1024)
LARGE = pltpu.CompilerParams(vmem_limit_bytes=20 * 1024 * 1024)


def ones_below(rows):
    return (
        lax.broadcasted_iota(jnp.int32, (rows, rows), 0)
        >= lax.broadcasted_iota(jnp.int32, (rows, rows), 1)
    ).astype(BF16)


def dot(a, b, ca, cb):
    return lax.dot_general(a, b, (((ca,), (cb,)), ((), ())), preferred_element_type=F32)


def within_rows(decay_t):
    return dot(decay_t, ones_below(decay_t.shape[1]), 1, 1)


def within_cols(decay_t):
    return dot(ones_below(decay_t.shape[1]), decay_t, 1, 1)


def parts_of(total):
    row = lax.broadcasted_iota(jnp.int32, (PAD, HD), 0)
    whole = jnp.broadcast_to(total, (PAD, HD))
    high = whole.astype(BF16).astype(F32)
    middle = (whole - high).astype(BF16).astype(F32)
    low = whole - high - middle
    parts = jnp.where(row == 0, high, jnp.where(row == 1, middle, jnp.where(row == 2, low, 0.0)))
    return parts.astype(BF16)


def total_of(ref, i):
    parts = ref[i, ref.shape[1] - PAD :, :].astype(F32)
    return parts[0:1, :] + parts[1:2, :] + parts[2:3, :]


def spread_kernel(weight_ref, out_ref):
    for i in range(out_ref.shape[0]):
        out_ref[i] = weight_ref[...]


def merge_kernel(in_ref, out_ref, work_ref, sems):
    count = sems.shape[0]
    rows = out_ref.shape[0] // count

    def copy(n):
        part = pl.ds(n * rows, rows)
        return pltpu.make_async_copy(work_ref.at[part], out_ref.at[part], sems.at[n])

    for n in range(count):
        for row in range(n * rows, (n + 1) * rows, 8):
            pair = jnp.concatenate([in_ref[row // 4], in_ref[row // 4 + 1]], axis=0)
            work_ref[row : row + 8, :] = pair
        copy(n).start()
    for n in range(count):
        copy(n).wait()


def pack_kernel(core_ref, plane_ref, line_ref, decay_ref, queries_ref, keys_ref, values_ref, own_ref, other_ref):
    first = core_ref[0] == 0
    half = (own_ref.shape[0] - 1) // 3
    place = lax.broadcasted_iota(jnp.int32, (HD, HD), 1)
    source = lax.broadcasted_iota(jnp.int32, (HD, HD), 0)
    wanted = (place // 64) * 64 + (place % 32 // 4) * 8 + (place // 32 % 2) * 4 + place % 4
    reorder = (source == wanted).astype(BF16)
    for n, ref in enumerate((keys_ref, values_ref, queries_ref)):
        for h in range(half):
            low = ref[:, h * HD : (h + 1) * HD]
            high = ref[:, (half + h) * HD : (half + h + 1) * HD]
            if ref is values_ref:
                low = dot(low, reorder, 1, 0).astype(BF16)
                high = dot(high, reorder, 1, 0).astype(BF16)
            own_ref[n * half + h] = jnp.where(first, low, high)
            other_ref[n * half + h] = jnp.where(first, high, low)
    low = decay_ref[:half, :].astype(F32)
    high = decay_ref[half:, :].astype(F32)
    rest = jnp.zeros((HD - half, HD), F32)
    kept = jnp.concatenate([jnp.where(first, low, high), rest], axis=0)
    sent = jnp.concatenate([jnp.where(first, high, low), rest], axis=0)
    own_ref[3 * half] = kept.astype(BF16)
    other_ref[3 * half] = sent.astype(BF16)


def both(first, own_ref, other_ref, i):
    own, other = own_ref[i], other_ref[i]
    return jnp.where(first, own, other), jnp.where(first, other, own)


def tokens(first, own_ref, other_ref, i):
    return jnp.concatenate(both(first, own_ref, other_ref, i), axis=0)


def decays(first, own_ref, other_ref):
    half = (own_ref.shape[0] - 1) // 3
    early, late = both(first, own_ref, other_ref, 3 * half)
    return jnp.concatenate([early[:half, :], late[:half, :]], axis=1)


def states_kernel(core_ref, own_ref, other_ref, out_ref):
    first = core_ref[0] == 0
    heads = (own_ref.shape[0] - 1) // 3
    pieces = out_ref.shape[0] // heads
    rows = HD // pieces
    decay_t = decays(first, own_ref, other_ref)
    count = decay_t.shape[1]
    within = within_rows(decay_t)
    total = within[:, count - 1 : count]
    coef = jnp.exp(total - within)
    for h in range(heads):
        keys_t = tokens(first, own_ref, other_ref, h).astype(F32).T * coef[h : h + 1, :]
        values = tokens(first, own_ref, other_ref, heads + h)
        state = dot(keys_t.astype(BF16), values, 1, 0).astype(BF16)
        parts = parts_of(total[h : h + 1, :])
        for j in range(pieces):
            out_ref[h * pieces + j, :rows, :] = state[rows * j : rows * (j + 1), :]
            out_ref[h * pieces + j, rows:, :] = parts


def group_kernel(group_ref, out_ref):
    rows = group_ref.shape[1] - PAD
    state = jnp.zeros((rows, HD), F32)
    total = jnp.zeros((1, HD), F32)
    for i in range(group_ref.shape[0]):
        step = total_of(group_ref, i)
        state = jnp.exp(step) * state + group_ref[i, :rows, :].astype(F32)
        total = total + step
    state = state.astype(BF16)
    parts = parts_of(total)
    for j in range(out_ref.shape[0]):
        out_ref[j, :rows, :] = state
        out_ref[j, rows:, :] = parts


def prior_kernel(plane_ref, line_ref, planes_ref, lines_ref, group_ref, out_ref):
    rows = out_ref.shape[1]
    state = jnp.zeros((rows, HD), F32)
    for place_ref, ref in ((plane_ref, planes_ref), (line_ref, lines_ref)):
        for i in range(ref.shape[0]):
            later = jnp.exp(total_of(ref, i)) * state + ref[i, :rows, :].astype(F32)
            state = jnp.where(i < place_ref[0], later, state)
    for i in range(group_ref.shape[0]):
        out_ref[i] = state.astype(BF16)
        state = jnp.exp(total_of(group_ref, i)) * state + group_ref[i, :rows, :].astype(F32)


def local_kernel(core_ref, own_ref, other_ref, out_ref, scale_ref):
    first = core_ref[0] == 0
    heads, count, _ = out_ref.shape
    decay_t = decays(first, own_ref, other_ref)
    rows = within_rows(decay_t)
    cols = within_cols(decay_t)
    scale_ref[...] = jnp.exp(cols)
    causal = lax.broadcasted_iota(jnp.int32, (count, count), 0) >= lax.broadcasted_iota(
        jnp.int32, (count, count), 1
    )
    for h in range(heads):
        keys = tokens(first, own_ref, other_ref, h)
        values = tokens(first, own_ref, other_ref, heads + h)
        queries = tokens(first, own_ref, other_ref, 2 * heads + h)
        scores = dot(queries, keys, 1, 1)
        gaps = cols[:, h : h + 1] - rows[h : h + 1, :]
        decay = jnp.exp(jnp.where(causal, gaps, -jnp.inf))
        weights = (scores * decay).astype(BF16)
        out_ref[h] = dot(weights, values, 1, 0)


def norm_kernel(
    core_ref, own_ref, other_ref, local_ref, scale_ref, prior_ref, keep_ref, send_ref
):
    first = core_ref[0] == 0
    heads = local_ref.shape[0]
    count = keep_ref.shape[1]
    scale = scale_ref[...]
    for h in range(heads):
        queries = tokens(first, own_ref, other_ref, 2 * heads + h)
        carried = dot(queries, prior_ref[h], 1, 0) * scale[:, h : h + 1]
        combined = local_ref[h] + carried
        square = jnp.mean(combined * combined, axis=-1, keepdims=True)
        normed = (combined * lax.rsqrt(square + 1e-05)).astype(BF16)
        keep_ref[h] = jnp.where(first, normed[:count], normed[count:])
        send_ref[h] = jnp.where(first, normed[count:], normed[:count])


def project_kernel(core_ref, kept_ref, got_ref, weight_ref, out_ref, rows_ref, sems):
    first = core_ref[0] == 0
    heads = rows_ref.shape[0]
    half = heads // 2
    lines = weight_ref.shape[0]

    def copy(h):
        source = weight_ref.at[h % lines, :, h // lines]
        return pltpu.make_async_copy(source, rows_ref.at[h], sems.at[h])

    def normed(h):
        low, high = both(first, kept_ref, got_ref, h % half)
        return low if h < half else high

    for h in range(heads):
        copy(h).start()
    acc = jnp.zeros(out_ref.shape, F32)
    for h in range(0, heads, RUN):
        run = range(h, h + RUN)
        for i in run:
            copy(i).wait()
        rows = rows_ref[h : h + RUN].reshape(RUN * HD, out_ref.shape[1])
        acc = acc + dot(jnp.concatenate([normed(i) for i in run], axis=1), rows, 1, 0)
    out_ref[...] = acc.astype(BF16)


def swap(x, within):
    return lax.all_to_all(
        x, ("seq", "head"), split_axis=0, concat_axis=0, axis_index_groups=within, tiled=True
    )


def shape(*dims, kind=F32):
    return jax.ShapeDtypeStruct(dims, kind)


def summed(group, copies):
    return pl.pallas_call(
        group_kernel,
        out_shape=shape(copies, *group.shape[1:], kind=BF16),
        compiler_params=VMEM,
    )(group)


def call(kernel, out, *args, **options):
    vmem = pl.BlockSpec(memory_space=pltpu.VMEM)
    smem = pl.BlockSpec(memory_space=pltpu.SMEM)
    return pl.pallas_call(
        kernel,
        out_shape=out,
        in_specs=[smem if a.dtype == jnp.int32 else vmem for a in args],
        out_specs=jax.tree.map(lambda _: vmem, out),
        compiler_params=VMEM,
        **options,
    )(*args)


def mix(queries, keys, values, log_decay, out_weight):
    count, width = queries.shape
    heads = log_decay.shape[1]
    half = heads // 2
    groups = lax.axis_size("seq")
    members = lax.axis_size("head")
    decay_t = log_decay.T
    devices = groups * members
    size = 2 * NEAR
    rows = HD * half // NEAR
    near = [list(range(i + c, i + size, 2)) for i in range(0, devices, size) for c in range(2)]
    lanes = groups // ROW
    chips = members // 2

    def device(x, y, z, c):
        return (x * ROW + y) * members + 2 * z + c

    plane = [
        [device(x, y, z, c) for x in range(lanes) for z in range(chips)]
        for y in range(ROW)
        for c in range(2)
    ]
    ring = [
        [device(x, y, z, c) for y in range(ROW) for c in range(2)]
        for x in range(lanes)
        for z in range(chips)
    ]
    pairs = size // members
    far = [
        [device(x, pairs * i + y, z, c) for i in range(ROW // pairs)]
        for x in range(lanes)
        for y in range(pairs)
        for z in range(chips)
        for c in range(2)
    ]
    across = [
        [device(x, y, z, c) for x in range(lanes)]
        for y in range(ROW)
        for z in range(chips)
        for c in range(2)
    ]
    partner = [(i, i ^ 1) for i in range(members)]
    seq = lax.axis_index("seq")
    core = lax.rem(lax.axis_index("head"), 2)
    core = core.reshape(1)
    plane_place = lax.div(seq, ROW).reshape(1)
    line_place = lax.div(lax.rem(seq, ROW), pairs).reshape(1)
    places = (plane_place, line_place)

    weight_rows = out_weight.shape[0]
    spread = pl.pallas_call(
        spread_kernel, out_shape=shape(groups, weight_rows, width, kind=BF16), compiler_params=VMEM
    )(out_weight)
    spread = swap(spread, plane)
    spread = pl.pallas_call(
        merge_kernel,
        out_shape=pltpu.HBM((groups * weight_rows, width), BF16),
        out_specs=pl.BlockSpec(memory_space=pltpu.HBM),
        scratch_shapes=[
            pltpu.VMEM((groups * weight_rows, width), BF16),
            pltpu.SemaphoreType.DMA((4,)),
        ],
        compiler_params=VMEM,
    )(spread)
    weight = lax.all_gather(
        spread, ("seq", "head"), axis=0, axis_index_groups=ring, tiled=True
    )

    pair = shape(3 * half + 1, count, HD, kind=BF16)
    own, other = call(pack_kernel, (pair, pair), core, *places, decay_t, queries, keys, values)
    other = lax.ppermute(other, "head", partner)
    states = call(states_kernel, shape(NEAR, rows + PAD, HD, kind=BF16), core, own, other)
    parts = (shape(half, 2 * count, HD), shape(2 * count, half))
    local_part, scale = call(local_kernel, parts, core, own, other)
    group = swap(states, near)
    lines = swap(summed(group, len(far[0])), far)
    planes = swap(summed(lines, lanes), across)
    prior = call(prior_kernel, shape(NEAR, rows, HD, kind=BF16), *places, planes, lines, group)
    prior = swap(prior, near).reshape(half, HD, HD)
    normed = shape(half, count, HD, kind=BF16)
    kept, sent = call(norm_kernel, (normed, normed), core, own, other, local_part, scale, prior)
    got = lax.ppermute(sent, "head", partner)
    run = chips * weight_rows
    weight = weight.reshape(ROW // 2, 4, lanes, run, width)
    weight = pltpu.with_memory_space_constraint(weight, pltpu.HBM)
    vmem = pl.BlockSpec(memory_space=pltpu.VMEM)
    return pl.pallas_call(
        project_kernel,
        out_shape=shape(count, width, kind=BF16),
        in_specs=[
            pl.BlockSpec(memory_space=pltpu.SMEM),
            vmem,
            vmem,
            pl.BlockSpec(memory_space=pltpu.HBM),
        ],
        out_specs=vmem,
        scratch_shapes=[
            pltpu.VMEM((heads, 4, run, width), BF16),
            pltpu.SemaphoreType.DMA((heads,)),
        ],
        compiler_params=LARGE,
    )(core, kept, got, weight)


def solution(mesh):
    placed = P(("seq", "head"), None)
    return jax.shard_map(mix, mesh=mesh, in_specs=(placed,) * 5, out_specs=placed, check_vma=False)
```
